32 devices in a mesh: dp: 8 (over z, x), fsdp: 4 (over y, core).
Axes of the slice: x: 2, y: 2, z: 4, core: 2. Of those that a mesh axis runs over, the one named last changes fastest.
Arguments:
- tokens: bfloat16 [8, 1, 64, 64, 768], P('dp', None, 'fsdp'), may hold values from -6 to 6
- cotangent: bfloat16 [8, 1, 64, 64, 768], P('dp', None, 'fsdp'), may hold values from -6 to 6
- size_tags: int32 [8, 1], P('dp'), may hold values from 0 to 1
- step_ids: int32 [8, 1, 4], P('dp'), may hold values from 0 to 999
- ada_weight: bfloat16 [768, 4608], P(('dp', 'fsdp')), may hold values from -0.3125 to 0.3125
- ada_bias: bfloat16 [4608], P(('dp', 'fsdp')), may hold values from -3 to 3
- attn_kernel: bfloat16 [9, 768], P(None, ('dp', 'fsdp')), may hold values from -2 to 2
- attn_shift: bfloat16 [768], P(('dp', 'fsdp')), may hold values from -3 to 3
- qkv_weight: bfloat16 [768, 2304], P(('dp', 'fsdp')), may hold values from -0.21875 to 0.21875
- qv_bias: bfloat16 [2, 768], P(None, ('dp', 'fsdp')), may hold values from -3 to 3
- out_weight: bfloat16 [768, 768], P(('dp', 'fsdp')), may hold values from -1.75 to 1.75
- out_bias: bfloat16 [768], P(('dp', 'fsdp')), may hold values from -3 to 3
- up_weight: bfloat16 [768, 3072], P(('dp', 'fsdp')), may hold values from -0.21875 to 0.21875
- up_bias: bfloat16 [3072], P(('dp', 'fsdp')), may hold values from -3 to 3
- ffn_kernel: bfloat16 [9, 3072], P(None, ('dp', 'fsdp')), may hold values from -2 to 2
- ffn_shift: bfloat16 [3072], P(('dp', 'fsdp')), may hold values from -3 to 3
- down_weight: bfloat16 [3072, 768], P(('dp', 'fsdp')), may hold values from -0.109375 to 0.109375
- down_bias: bfloat16 [768], P(('dp', 'fsdp')), may hold values from -3 to 3
Outputs:
- block_out: bfloat16 [8, 1, 64, 64, 768], P('dp', None, 'fsdp')
- grad_tokens: bfloat16 [8, 1, 64, 64, 768], P('dp', None, 'fsdp')
- grad_ada_weight: float32 [768, 4608], P(('dp', 'fsdp'))
- grad_ada_bias: float32 [4608], P(('dp', 'fsdp'))
- grad_attn_kernel: float32 [9, 768], P(None, ('dp', 'fsdp'))
- grad_attn_shift: float32 [768], P(('dp', 'fsdp'))
- grad_qkv_weight: float32 [768, 2304], P(('dp', 'fsdp'))
- grad_qv_bias: float32 [2, 768], P(None, ('dp', 'fsdp'))
- grad_out_weight: float32 [768, 768], P(('dp', 'fsdp'))
- grad_out_bias: float32 [768], P(('dp', 'fsdp'))
- grad_up_weight: float32 [768, 3072], P(('dp', 'fsdp'))
- grad_up_bias: float32 [3072], P(('dp', 'fsdp'))
- grad_ffn_kernel: float32 [9, 3072], P(None, ('dp', 'fsdp'))
- grad_ffn_shift: float32 [3072], P(('dp', 'fsdp'))
- grad_down_weight: float32 [3072, 768], P(('dp', 'fsdp'))
- grad_down_bias: float32 [768], P(('dp', 'fsdp'))
The draws below stay inside these ranges and needn't reach their ends.
Inputs may be any that keep to these rules, and one draw needn't show every extreme that they name: `size_tags`: 1 where a canvas holds one item of 64 x 64 tokens, 0 where its four quadrants are four items.
All inputs are finite; a program needn't handle non-finite values.
Results may differ from the reference program's by a relative error of at most 0.018.
Values may be sent and summed in bfloat16 or wider, within the bound.
No kernel may reach another device: no remote copies, remote signals or barrier semaphores. Data moves between devices by JAX's collectives and lax.ppermute only.
A program may use at most 384 MiB of HBM per device.

```python
import math
import jax
import jax.numpy as jnp
from jax import lax

D = 768
HEADS = 12
HDIM = 64
FF = 3072
GRID = 64
CANV = 1
N_DP = 8


def place_ends(values, key, low, high):
    longest = values.shape.index(max(values.shape))
    spots = []
    for shift in (0, 1):
        where = [jax.random.randint(jax.random.fold_in(key, axis), (), 0, length) for axis, length in enumerate(values.shape)]
        where[longest] = (where[longest] + shift) % values.shape[longest]
        spots.append(tuple(where))
    return values.at[spots[0]].set(low).at[spots[1]].set(high)


def shard_levels(stream_key, dims, pieces, smallest, largest):
    loudness, own = 1.0, jax.random.fold_in(stream_key, 6)
    for position, blocks in pieces:
        heights = jnp.exp(jax.random.uniform(jax.random.fold_in(own, position), (blocks,), jnp.float32, smallest / len(pieces), largest / len(pieces)))
        loudness = loudness * jnp.repeat(heights, dims[position] // blocks).reshape([-1 if axis == position else 1 for axis in range(len(dims))])
    return loudness


def noise(stream_key, dims, width, reach, shards=(), kind=jnp.bfloat16):
    array = width * jax.random.normal(stream_key, dims, jnp.float32)
    if shards:
        array = array * shard_levels(stream_key, dims, shards, -0.22, 0.18)
    return jnp.clip(array, -reach, reach).astype(kind)


def setup_inputs(seed: int = 0) -> dict:
    key_of = jax.random.split(jax.random.key(seed), 19)
    return {
        "tokens": noise(key_of[0], (N_DP, CANV, GRID, GRID, D), 1.0, 6.0, ((0, 8), (2, 4))),
        "cotangent": noise(key_of[1], (N_DP, CANV, GRID, GRID, D), 1.0, 6.0, ((0, 8), (2, 4))),
        "size_tags": place_ends(jax.random.randint(key_of[2], (N_DP, CANV), 0, 2), jax.random.fold_in(key_of[2], 1), 0, 1).astype(jnp.int32),
        "step_ids": place_ends(jax.random.randint(key_of[3], (N_DP, CANV, 4), 0, 1000), jax.random.fold_in(key_of[3], 1), 0, 999).astype(jnp.int32),
        "ada_weight": noise(key_of[4], (D, 6 * D), (D // 2) ** -0.5, 0.3125, ((0, 32),)),
        "ada_bias": noise(key_of[5], (6 * D,), 0.5, 3.0, ((0, 32),)),
        "attn_kernel": noise(key_of[6], (9, D), 9 ** -0.5, 2.0, ((1, 32),)),
        "attn_shift": noise(key_of[7], (D,), 0.5, 3.0, ((0, 32),)),
        "qkv_weight": noise(key_of[8], (D, 3 * D), D ** -0.5, 0.21875, ((0, 32),)),
        "qv_bias": noise(key_of[9], (2, D), 0.5, 3.0, ((1, 32),)),
        "out_weight": noise(key_of[10], (D, D), (D // 64) ** -0.5, 1.75, ((0, 32),)),
        "out_bias": noise(key_of[11], (D,), 0.5, 3.0, ((0, 32),)),
        "up_weight": noise(key_of[12], (D, FF), D ** -0.5, 0.21875, ((0, 32),)),
        "up_bias": noise(key_of[13], (FF,), 0.5, 3.0, ((0, 32),)),
        "ffn_kernel": noise(key_of[14], (9, FF), 9 ** -0.5, 2.0, ((1, 32),)),
        "ffn_shift": noise(key_of[15], (FF,), 0.5, 3.0, ((0, 32),)),
        "down_weight": noise(key_of[16], (FF, D), FF ** -0.5, 0.109375, ((0, 32),)),
        "down_bias": noise(key_of[17], (D,), 0.5, 3.0, ((0, 32),)),
    }


@jax.custom_vjp
def low(v):
    return lax.optimization_barrier(v.astype(jnp.bfloat16)).astype(jnp.float32)

@jax.custom_vjp
def low_back(v):
    return v

def low_keep(v):
    return (low(v), None)

def low_pass(kept, grad):
    return (grad,)

def back_keep(v):
    return (v, None)

def back_low(kept, grad):
    return (low(grad),)
low.defvjp(low_keep, low_pass)
low_back.defvjp(back_keep, back_low)

def layer_norm(values):
    centre = values - lax.optimization_barrier(jnp.mean(values, axis=-1, keepdims=True))
    spread = lax.optimization_barrier(jnp.mean(centre * centre, axis=-1, keepdims=True))
    return centre * lax.rsqrt(spread + 1e-06)

def embed_steps(chosen):
    half_width = D // 2
    frequency = jnp.exp(-math.log(10000.0) * jnp.arange(half_width, dtype=jnp.float32) / half_width)
    angles = chosen.astype(jnp.float32)[..., None] * frequency
    return jnp.concatenate([jnp.cos(angles), jnp.sin(angles)], axis=-1)

def quadrant_map(values):
    channels = values.shape[-1]
    blocks = values.reshape(2, 1, 2, 1, channels)
    spread_out = jnp.broadcast_to(blocks, (2, GRID // 2, 2, GRID // 2, channels))
    return spread_out.reshape(GRID, GRID, channels)

def depthwise(values, kernel, shift_bias, big_item):
    coords = jnp.arange(GRID)
    lower_half = coords >= GRID // 2
    tap_masks = []
    for offset in (-1, 0, 1):
        moved_half = coords + offset >= GRID // 2
        tap_masks.append(jnp.logical_or(big_item, moved_half == lower_half).astype(jnp.float32))
    padded = jnp.pad(values, ((1, 1), (1, 1), (0, 0)))
    summed = jnp.zeros(values.shape, jnp.float32) + shift_bias
    for row_off in (-1, 0, 1):
        for col_off in (-1, 0, 1):
            tap_index = (row_off + 1) * 3 + col_off + 1
            window = padded[1 + row_off:1 + row_off + GRID, 1 + col_off:1 + col_off + GRID]
            gate_mask = tap_masks[row_off + 1][:, None, None] * tap_masks[col_off + 1][None, :, None]
            summed = summed + window * kernel[tap_index] * gate_mask
    return summed

def canvas_forward(weights_in, block):
    ada_weight, ada_bias, attn_kernel, attn_shift, qkv_weight, qv_bias, out_weight, out_bias, up_weight, up_bias, ffn_kernel, ffn_shift, down_weight, down_bias = weights_in
    canvas_tokens, big_flag, quad_steps = block
    high = lax.Precision.HIGHEST
    big_item = big_flag == 1
    chosen = jnp.where(big_item, quad_steps[0], quad_steps)
    embedded = low(jax.nn.silu(embed_steps(chosen)))
    modulation = jnp.dot(embedded, ada_weight, precision=high) + ada_bias
    shift_one, scale_one, gate_one, shift_two, scale_two, gate_two = [quadrant_map(modulation[:, piece_index * D:(piece_index + 1) * D]) for piece_index in range(6)]
    normed_one = layer_norm(canvas_tokens)
    first = low(normed_one * (1.0 + scale_one) + shift_one)
    mixed = low(low_back(depthwise(first, attn_kernel, attn_shift, big_item)))
    bias_row = jnp.concatenate([qv_bias[0], jnp.zeros((D,), jnp.float32), qv_bias[1]])
    projected = jnp.dot(mixed.reshape(GRID * GRID, D), qkv_weight, precision=high) + bias_row
    grouped = projected.reshape(GRID // 2, 2, GRID // 2, 2, 3 * D).transpose(1, 3, 0, 2, 4)
    grouped = grouped.reshape(4, GRID * GRID // 4, 3, HEADS, HDIM)
    queries = low(low_back(grouped[:, :, 0]))
    keys_all = low(low_back(grouped[:, :, 1]))
    values_all = low(low_back(grouped[:, :, 2]))
    scores = low_back(jnp.einsum('pqhd,pkhd->phqk', queries, keys_all, precision=high) * HDIM ** (-0.5))
    side_flag = (jnp.arange(GRID // 2) >= GRID // 4).astype(jnp.int32)
    quadrant = (2 * side_flag[:, None] + side_flag[None, :]).reshape(-1)
    allowed = jnp.logical_or(big_item, quadrant[:, None] == quadrant[None, :])
    scores = jnp.where(allowed, scores, -1e+30)
    weights = jax.nn.softmax(scores, axis=-1)
    attended = low(low_back(jnp.einsum('phqk,pkhd->pqhd', low(weights), values_all, precision=high)))
    merged = attended.reshape(2, 2, GRID // 2, GRID // 2, D).transpose(2, 0, 3, 1, 4).reshape(GRID * GRID, D)
    branch_one = low_back(jnp.dot(merged, out_weight, precision=high) + out_bias)
    hidden_state = canvas_tokens + gate_one * branch_one.reshape(GRID, GRID, D)
    normed_two = layer_norm(hidden_state)
    second = low(normed_two * (1.0 + scale_two) + shift_two)
    expanded = low(low_back(jnp.dot(second.reshape(GRID * GRID, D), up_weight, precision=high) + up_bias))
    convolved = low_back(depthwise(expanded.reshape(GRID, GRID, FF), ffn_kernel, ffn_shift, big_item))
    activated = low(jax.nn.gelu(convolved, approximate=True))
    branch_two = low_back(jnp.dot(activated.reshape(GRID * GRID, FF), down_weight, precision=high) + down_bias)
    return hidden_state + gate_two * branch_two.reshape(GRID, GRID, D)

def reference(tokens, cotangent, size_tags, step_ids, ada_weight, ada_bias, attn_kernel, attn_shift, qkv_weight, qv_bias, out_weight, out_bias, up_weight, up_bias, ffn_kernel, ffn_shift, down_weight, down_bias):
    params = tuple((weight_arg.astype(jnp.float32) for weight_arg in (ada_weight, ada_bias, attn_kernel, attn_shift, qkv_weight, qv_bias, out_weight, out_bias, up_weight, up_bias, ffn_kernel, ffn_shift, down_weight, down_bias)))
    flat_tokens = tokens.astype(jnp.float32).reshape(N_DP * CANV, GRID, GRID, D)
    flat_tags = size_tags.reshape(N_DP * CANV)
    flat_steps = step_ids.reshape(N_DP * CANV, 4)

    def forward(token_grid, weights_in):

        def one_canvas(carry, block):
            return (carry, canvas_forward(weights_in, block))
        unused_carry, outputs = lax.scan(jax.checkpoint(one_canvas), jnp.zeros((), jnp.float32), (token_grid, flat_tags, flat_steps))
        return outputs
    result, pullback = jax.vjp(forward, flat_tokens, params)
    grad_flat, grad_params = pullback(cotangent.astype(jnp.float32).reshape(flat_tokens.shape))
    return (result.reshape(tokens.shape).astype(jnp.bfloat16), grad_flat.reshape(tokens.shape).astype(jnp.bfloat16), grad_params[0], grad_params[1], grad_params[2], grad_params[3], grad_params[4], grad_params[5], grad_params[6], grad_params[7], grad_params[8], grad_params[9], grad_params[10], grad_params[11], grad_params[12], grad_params[13])
```

```python
import functools
import math

import jax
import jax.numpy as jnp
from jax import lax
from jax.experimental import pallas as pl
from jax.experimental.pallas import tpu as pltpu
from jax.sharding import PartitionSpec as P

HEADS = 12
HDIM = 64
EVERY = ("dp", "fsdp")
F32 = jnp.float32
BF16 = jnp.bfloat16


def bits_of(axis):
    size = lax.axis_size(axis)
    count = size.bit_length() - 1
    assert 1 << count == size, axis
    return [(axis, 1 << k) for k in range(count)]


def my_bit(axis, bit):
    return (lax.axis_index(axis) // bit) % 2


def swap(value, axis, bit):
    size = lax.axis_size(axis)
    return lax.ppermute(value, axis, [(i, i ^ bit) for i in range(size)])


def by_bit(mine, other, flag, dim, join=jnp.stack):
    low = jnp.where(flag == 0, mine, other)
    high = jnp.where(flag == 0, other, mine)
    return join([low, high], axis=dim)


def halves(value, flag, dim):
    half = value.shape[dim] // 2
    keep = lax.dynamic_slice_in_dim(value, flag * half, half, axis=dim)
    give = lax.dynamic_slice_in_dim(value, (1 - flag) * half, half, axis=dim)
    return keep, give


def gather_small(value, bits):
    order = bits[::-1]
    for step, (axis, bit) in enumerate(order):
        value = by_bit(value, swap(value, axis, bit), my_bit(axis, bit), step)
    return value.reshape((1 << len(order),) + value.shape[len(order):])


def scatter_small(value, bits):
    sizes = [2] * len(bits)
    value = value.reshape(sizes + [value.shape[0] >> len(bits)] + list(value.shape[1:]))
    for step, (axis, bit) in enumerate(bits):
        dim = len(bits) - 1 - step
        flag = my_bit(axis, bit)
        keep, give = halves(value, flag, dim)
        value = keep + swap(give, axis, bit)
    return value.reshape(value.shape[len(bits):])


def exchange(blocks, axis):
    bits = bits_of(axis)
    value = blocks.reshape([2] * len(bits) + list(blocks.shape[1:]))
    for step, (name, bit) in enumerate(bits):
        dim = len(bits) - 1 - step
        flag = my_bit(name, bit)
        keep, give = halves(value, flag, dim)
        other = swap(give, name, bit)
        value = by_bit(keep, other, flag, dim, jnp.concatenate)
    return value.reshape(blocks.shape)


def with_halo(cells, axis, dim, width):
    count = lax.axis_size(axis)
    ends = count - 1
    head = lax.slice_in_dim(cells, 0, width, axis=dim)
    tail = lax.slice_in_dim(cells, cells.shape[dim] - width, cells.shape[dim], axis=dim)
    above = lax.ppermute(tail, axis, [(i, i + 1) for i in range(ends)])
    below = lax.ppermute(head, axis, [(i + 1, i) for i in range(ends)])
    return above, below


def layer_norm(values):
    centre = values - jnp.mean(values, axis=-1, keepdims=True)
    spread = jnp.mean(centre * centre, axis=-1, keepdims=True)
    rate = lax.rsqrt(spread + 1e-06)
    return centre * rate, rate


def layer_norm_back(grad, normed, rate):
    mean_grad = jnp.mean(grad, axis=-1, keepdims=True)
    mean_both = jnp.mean(grad * normed, axis=-1, keepdims=True)
    return rate * (grad - mean_grad - normed * mean_both)


def split_cols(values):
    shape = values.shape
    shaped = values.reshape(shape[:-2] + (shape[-2] // 2, 2, shape[-1]))
    return jnp.swapaxes(shaped, -3, -2)


def join_cols(values):
    shape = values.shape
    return jnp.swapaxes(values, -3, -2).reshape(shape[:-3] + (2 * shape[-2], shape[-1]))


def side_cells(cells, big):
    half = cells.shape[3]
    even, odd = cells[:, :, 0], cells[:, :, 1]
    spot = jnp.arange(half)[None, None, :, None]
    same = big[:, None, None, None]
    pad = ((0, 0), (0, 0), (1, 1), (0, 0))
    odd_down = jnp.pad(odd, pad)[:, :, :half] * jnp.where(spot == half // 2, same, 1.0)
    even_up = jnp.pad(even, pad)[:, :, 2:] * jnp.where(spot == half // 2 - 1, same, 1.0)
    left = jnp.stack([odd_down, even], axis=2)
    right = jnp.stack([odd, even_up], axis=2)
    return left, right


def conv(cells, kernel, big):
    cells = cells.astype(F32)
    rows = cells.shape[1] - 2
    left, right = side_cells(cells, big)
    total = 0.0
    for down in range(3):
        for across, part in enumerate((left, cells, right)):
            total = total + part[:, down : down + rows] * kernel[3 * down + across]
    return total


def tap_grads(cells, grads, big):
    cells = cells.astype(F32)
    rows = cells.shape[1] - 2
    left, right = side_cells(cells, big)
    sums = []
    for down in range(3):
        for part in (left, cells, right):
            sums.append(jnp.sum(part[:, down : down + rows] * grads, axis=(0, 1, 2, 3)))
    return jnp.stack(sums)


def item_sums(values):
    half = values.shape[3] // 2
    shaped = values.reshape(values.shape[:3] + (2, half, values.shape[-1]))
    return shaped.sum(axis=(1, 2, 4))


def spread_items(piece, grid):
    return jnp.repeat(piece, grid // 4, axis=1)[:, None, None]


def contract_rows(left_side, right_side):
    return lax.dot_general(
        left_side, right_side, (((0,), (0,)), ((), ())), preferred_element_type=F32
    )


def contract_cols(left_side, right_side):
    return lax.dot_general(
        left_side, right_side, (((1,), (1,)), ((), ())), preferred_element_type=F32
    )


def matmul(left_side, right_side):
    return jnp.dot(left_side, right_side, preferred_element_type=F32)


GELU_C = math.sqrt(2.0 / math.pi)
GELU_A = 0.044715


def shifted(values, mask, step):
    lead = values.shape[0] * 8
    flat = values.reshape(lead, values.shape[2])
    return pltpu.roll(flat, step % lead, axis=0).reshape(values.shape) * mask


def conv_row(load, taps):
    even_sum = odd_sum = None
    for down in range(3):
        even, odd, odd_down, even_up = load(down)
        left, centre, right = taps[3 * down : 3 * down + 3]
        even_part = left * odd_down + centre * even + right * odd
        odd_part = left * even + centre * odd + right * even_up
        even_sum = even_part if even_sum is None else even_sum + even_part
        odd_sum = odd_part if odd_sum is None else odd_sum + odd_part
    return even_sum, odd_sum


def ffn_body(canvases, rows, half, lanes, flag_ref, second_ref, grad_ref, up_ref, up_bias_ref, kernel_ref, shift_ref,
             down_ref, branch_ref, grad_second_ref, grad_up_ref, grad_down_ref, sums_ref,
             cells, cells_side, grads, grads_side, active, grad_cells, second_t):
    step = pl.program_id(0)
    width = second_ref.shape[1]
    block = up_ref.shape[1]
    grid = 2 * half
    group = half // 8
    tile = 256
    ext = rows + 4
    mid = rows + 2
    own = rows * grid

    @pl.when(step == 0)
    def _():
        branch_ref[...] = jnp.zeros_like(branch_ref)
        grad_second_ref[...] = jnp.zeros_like(grad_second_ref)
        for c in range(canvases):
            start = (c * ext + 2) * grid
            second_t[:, c * own : (c + 1) * own] = second_ref[start : start + own, :].T

    spot = lax.broadcasted_iota(jnp.int32, (group, 8, lanes), 0) * 8 + lax.broadcasted_iota(jnp.int32, (group, 8, lanes), 1)

    def masks(c):
        big = flag_ref[c, 0]
        down_mask = jnp.where(spot == 0, 0.0, jnp.where(spot == half // 2, big, 1.0))
        up_mask = jnp.where(spot == half - 1, 0.0, jnp.where(spot == half // 2 - 1, big, 1.0))
        return down_mask, up_mask

    @pl.loop(0, block // tile)
    def _(n):
        cols = pl.ds(pl.multiple_of(n * tile, tile), tile)
        product = matmul(second_ref[...], up_ref[:, cols]) + up_bias_ref[:, cols]
        cells[:, :, cols] = product.reshape(-1, 8, tile)
        weight = down_ref[pl.ds(pl.multiple_of(n * tile, tile), tile), :]
        grads[:, :, cols] = contract_cols(grad_ref[...], weight).reshape(-1, 8, tile)

    for c in range(canvases):
        @pl.when(flag_ref[c, 1] == 0)
        def _():
            cells[pl.ds(c * ext * grid // 8, 2 * grid // 8)] = jnp.zeros((2 * grid // 8, 8, block), F32)

        @pl.when(flag_ref[c, 2] == 0)
        def _():
            cells[pl.ds(((c + 1) * ext - 2) * grid // 8, 2 * grid // 8)] = jnp.zeros((2 * grid // 8, 8, block), F32)

    chunks = block // lanes
    per_row = grid // 8

    for c in range(canvases):
        down_mask, up_mask = masks(c)

        @pl.loop(0, ext)
        def _(r):
            base = (c * ext + r) * per_row
            for k in range(chunks):
                cols = slice(k * lanes, (k + 1) * lanes)
                even = cells[pl.ds(base, group), :, cols]
                odd = cells[pl.ds(base + group, group), :, cols]
                cells_side[pl.ds(base, group), :, cols] = shifted(odd, down_mask, 1)
                cells_side[pl.ds(base + group, group), :, cols] = shifted(even, up_mask, -1)

        @pl.loop(0, chunks)
        def _(k):
            cols = pl.ds(pl.multiple_of(k * lanes, lanes), lanes)
            taps = [kernel_ref[pl.ds(t, 1), cols][None] for t in range(9)]
            taps = [jnp.broadcast_to(t, (1, 8, lanes)) for t in taps]
            shift = jnp.broadcast_to(shift_ref[:, cols][None], (1, 8, lanes))

            @pl.loop(0, mid)
            def _(r):
                def load(down):
                    base = (c * ext + r + down) * per_row
                    return (cells[pl.ds(base, group), :, cols], cells[pl.ds(base + group, group), :, cols],
                            cells_side[pl.ds(base, group), :, cols], cells_side[pl.ds(base + group, group), :, cols])

                sums = conv_row(load, taps)
                here = (c * mid + r) * per_row
                outs = []
                for side in range(2):
                    v = sums[side] + shift
                    square = v * v
                    t = jnp.tanh(v * (GELU_C + (GELU_C * GELU_A) * square))
                    gate = 0.5 + 0.5 * t
                    slope = gate + (v * (2 * GELU_C + (6 * GELU_C * GELU_A) * square)) * (gate - gate * gate)
                    spots = pl.ds(here + side * group, group)
                    active[spots, :, cols] = (v * gate).astype(BF16)
                    outs.append(grads[spots, :, cols] * slope)
                    grads[spots, :, cols] = outs[-1]
                grads_side[pl.ds(here, group), :, cols] = shifted(outs[1], down_mask, 1)
                grads_side[pl.ds(here + group, group), :, cols] = shifted(outs[0], up_mask, -1)

        for row, flag in ((0, 1), (mid - 1, 2)):
            @pl.when(flag_ref[c, flag] == 0)
            def _():
                spots = pl.ds((c * mid + row) * per_row, per_row)
                grads[spots] = jnp.zeros((per_row, 8, block), F32)
                grads_side[spots] = jnp.zeros((per_row, 8, block), F32)

        @pl.loop(0, chunks)
        def _(k):
            cols = pl.ds(pl.multiple_of(k * lanes, lanes), lanes)
            taps = [kernel_ref[pl.ds(8 - t, 1), cols][None] for t in range(9)]
            taps = [jnp.broadcast_to(t, (1, 8, lanes)) for t in taps]

            def row_step(r, sums):
                def load_grads(down):
                    base = (c * mid + r + down) * per_row
                    return (grads[pl.ds(base, group), :, cols], grads[pl.ds(base + group, group), :, cols],
                            grads_side[pl.ds(base, group), :, cols], grads_side[pl.ds(base + group, group), :, cols])

                back_even, back_odd = conv_row(load_grads, taps)
                here = (c * rows + r) * per_row
                grad_cells[pl.ds(here, group), :, cols] = back_even.astype(BF16)
                grad_cells[pl.ds(here + group, group), :, cols] = back_odd.astype(BF16)
                mine = (c * mid + r + 1) * per_row
                g_even = grads[pl.ds(mine, group), :, cols]
                g_odd = grads[pl.ds(mine + group, group), :, cols]
                new = []
                for down in range(3):
                    base = (c * ext + r + 1 + down) * per_row
                    even = cells[pl.ds(base, group), :, cols]
                    odd = cells[pl.ds(base + group, group), :, cols]
                    odd_down = cells_side[pl.ds(base, group), :, cols]
                    even_up = cells_side[pl.ds(base + group, group), :, cols]
                    for for_even, for_odd in ((odd_down, even), (even, odd), (odd, even_up)):
                        new.append(jnp.sum(for_even * g_even + for_odd * g_odd, axis=0))
                new.append(jnp.sum(g_even + g_odd, axis=0))
                new.append(jnp.sum(back_even + back_odd, axis=0))
                return tuple(s + v for s, v in zip(sums, new))

            zero = jnp.zeros((8, lanes), F32)
            sums = lax.fori_loop(0, rows, row_step, (zero,) * 11)
            for t in range(11):
                total = jnp.sum(sums[t], axis=0, keepdims=True)
                if c == 0:
                    sums_ref[pl.ds(t, 1), cols] = total
                else:
                    sums_ref[pl.ds(t, 1), cols] += total

    for c in range(canvases):
        mine = slice(c * own, (c + 1) * own)
        act_rows = pl.ds((c * mid + 1) * per_row, rows * per_row)
        own_grad = grad_ref[(c * mid + 1) * grid : (c * mid + 1) * grid + own, :]

        @pl.loop(0, width // tile)
        def _(n):
            cols = pl.ds(pl.multiple_of(n * tile, tile), tile)
            branch_ref[mine, cols] += matmul(active[act_rows].reshape(own, block), down_ref[:, cols])
            weight = up_ref[pl.ds(pl.multiple_of(n * tile, tile), tile), :]
            spots = pl.ds(c * rows * per_row, rows * per_row)
            grad_second_ref[mine, cols] += contract_cols(grad_cells[spots].reshape(own, block), weight)

        @pl.loop(0, block // tile)
        def _(n):
            cols = pl.ds(pl.multiple_of(n * tile, tile), tile)
            part = contract_rows(active[act_rows, :, cols].reshape(own, tile), own_grad)
            if canvases == 1:
                grad_down_ref[cols, :] = part.astype(grad_down_ref.dtype)
            elif c == 0:
                grad_down_ref[cols, :] = part.astype(grad_down_ref.dtype)
            else:
                grad_down_ref[cols, :] += part.astype(grad_down_ref.dtype)

    @pl.loop(0, block // tile)
    def _(n):
        cols = pl.ds(pl.multiple_of(n * tile, tile), tile)
        grad_up_ref[:, cols] = matmul(second_t[...], grad_cells[:, :, cols].reshape(-1, tile)).astype(grad_up_ref.dtype)


def feed_forward(flags, second, grad_two, up, up_bias, kernel, shift, down, canvases, rows, half):
    width, hidden = up.shape
    block, lanes = 768, 128
    grid = 2 * half
    ext, mid, own = [canvases * n * grid for n in (rows + 4, rows + 2, rows)]
    kernel = jnp.pad(kernel, ((0, 7), (0, 0)))
    body = functools.partial(ffn_body, canvases, rows, half, lanes)
    fixed = lambda shape: pl.BlockSpec(shape, lambda i: (0, 0), pipeline_mode=pl.Buffered(1))
    cols = lambda n: pl.BlockSpec((n, block), lambda i: (0, i))
    return pl.pallas_call(
        body,
        grid=(hidden // block,),
        in_specs=[
            pl.BlockSpec(memory_space=pltpu.SMEM),
            fixed((ext, width)),
            fixed((mid, width)),
            cols(width),
            cols(1),
            cols(16),
            cols(1),
            pl.BlockSpec((block, width), lambda i: (i, 0)),
        ],
        out_specs=[
            pl.BlockSpec((own, width), lambda i: (0, 0)),
            pl.BlockSpec((own, width), lambda i: (0, 0)),
            cols(width),
            pl.BlockSpec((block, width), lambda i: (i, 0)),
            cols(16),
        ],
        out_shape=[
            jax.ShapeDtypeStruct((own, width), F32),
            jax.ShapeDtypeStruct((own, width), F32),
            jax.ShapeDtypeStruct((width, hidden), BF16),
            jax.ShapeDtypeStruct((hidden, width), BF16 if canvases == 1 else F32),
            jax.ShapeDtypeStruct((16, hidden), F32),
        ],
        scratch_shapes=[
            pltpu.VMEM((ext // 8, 8, block), F32),
            pltpu.VMEM((ext // 8, 8, block), F32),
            pltpu.VMEM((mid // 8, 8, block), F32),
            pltpu.VMEM((mid // 8, 8, block), F32),
            pltpu.VMEM((mid // 8, 8, block), BF16),
            pltpu.VMEM((own // 8, 8, block), BF16),
            pltpu.VMEM((width, own), BF16),
        ],
        compiler_params=pltpu.CompilerParams(vmem_limit_bytes=60 << 20, dimension_semantics=("arbitrary",)),
        cost_estimate=pl.CostEstimate(flops=36 * own * width * hidden // 3, bytes_accessed=40 << 20, transcendentals=own * hidden),
        name="feed_forward",
    )(flags, second, grad_two, up, up_bias[None], kernel, shift[None], down)


def one_head(pair, head):
    lane = lax.broadcasted_iota(jnp.int32, pair.shape, 1)
    return jnp.where((lane < HDIM) == (head == 0), pair, jnp.zeros_like(pair))


def attend_forward_body(tile, query_ref, key_ref, value_ref, query_item_ref, key_item_ref, out_ref, lse_ref, key_wide):
    tokens = query_ref.shape[0]
    pair = query_ref.shape[1]
    scale = HDIM ** -0.5
    key_wide[:, :pair] = key_ref[...]
    key_wide[:, pair:] = key_item_ref[...]

    @pl.loop(0, tokens // tile)
    def _(n):
        spots = pl.ds(pl.multiple_of(n * tile, tile), tile)
        query = query_ref[spots, :] * jnp.asarray(scale, BF16)
        outs = []
        for head in range(2):
            wide = jnp.concatenate([one_head(query, head), query_item_ref[spots, :]], axis=1)
            scores = contract_cols(wide, key_wide[...])
            top = jnp.max(scores, axis=1, keepdims=True)
            weights = jnp.exp(scores - top)
            total = jnp.sum(weights, axis=1, keepdims=True)
            outs.append(matmul(weights.astype(BF16), value_ref[...]) / total)
            lse = jnp.broadcast_to(top + jnp.log(total), (tile, 128))
            lse_ref[0, pl.ds(head, 1), spots] = lse.T[:1]
        lane = lax.broadcasted_iota(jnp.int32, outs[0].shape, 1)
        out_ref[spots, :] = jnp.where(lane < HDIM, outs[0], outs[1]).astype(BF16)


def attend_forward(projected, query_item, key_item):
    tokens = projected.shape[0]
    width = projected.shape[1] // 3
    pair = 2 * HDIM
    pairs = width // pair
    block = lambda k: pl.BlockSpec((tokens, pair), lambda i: (0, i + k * pairs))
    fixed = pl.BlockSpec((tokens, 128), lambda i: (0, 0))
    return pl.pallas_call(
        functools.partial(attend_forward_body, 256),
        grid=(pairs,),
        in_specs=[block(0), block(1), block(2), fixed, fixed],
        out_specs=[block(0), pl.BlockSpec((1, 8, tokens), lambda i: (i, 0, 0))],
        out_shape=[jax.ShapeDtypeStruct((tokens, width), BF16), jax.ShapeDtypeStruct((pairs, 8, tokens), F32)],
        scratch_shapes=[pltpu.VMEM((tokens, 2 * pair), BF16)],
        compiler_params=pltpu.CompilerParams(vmem_limit_bytes=40 << 20, dimension_semantics=("arbitrary",)),
        cost_estimate=pl.CostEstimate(flops=8 * tokens * tokens * width, bytes_accessed=8 << 20, transcendentals=tokens * tokens * width // HDIM),
        name="attend_forward",
    )(projected, projected, projected, query_item, key_item)


def attend_backward_body(tile, query_ref, key_ref, value_ref, query_item_ref, key_item_ref, grad_ref, out_ref, lse_ref,
                         result_ref, key_wide, key_t, query_t):
    tokens = query_ref.shape[0]
    pair = query_ref.shape[1]
    scale = HDIM ** -0.5
    key_wide[:, :pair] = key_ref[...]
    key_wide[:, pair:] = key_item_ref[...]
    key_t[...] = key_ref[...].T

    grad_key = [jnp.zeros((), F32)] * 2
    result_ref[1] = jnp.zeros_like(result_ref[1])
    result_ref[2] = jnp.zeros_like(result_ref[2])

    @pl.loop(0, tokens // tile)
    def _(n):
        spots = pl.ds(pl.multiple_of(n * tile, tile), tile)
        query = query_ref[spots, :] * jnp.asarray(scale, BF16)
        grad = grad_ref[spots, :]
        both = (grad.astype(F32) * out_ref[spots, :].astype(F32)).T
        keys_new = []
        values_new = []
        queries_new = []
        for head in range(2):
            own = slice(head * HDIM, (head + 1) * HDIM)
            centre = jnp.sum(both[own], axis=0, keepdims=True)
            wide = jnp.concatenate([one_head(query, head), query_item_ref[spots, :]], axis=1)
            weights = jnp.exp(contract_cols(key_wide[...], wide) - lse_ref[0, pl.ds(head, 1), spots])
            grad_weights = contract_cols(value_ref[...], one_head(grad, head))
            grad_scores = (weights * (grad_weights - centre)).astype(BF16)
            values_new.append(matmul(weights.astype(BF16), grad))
            keys_new.append(matmul(grad_scores, query))
            queries_new.append(matmul(key_t[...], grad_scores)[own])
        lane = lax.broadcasted_iota(jnp.int32, keys_new[0].shape, 1)
        result_ref[1] += jnp.where(lane < HDIM, keys_new[0], keys_new[1])
        result_ref[2] += jnp.where(lane < HDIM, values_new[0], values_new[1])
        query_t[:, spots] = jnp.concatenate(queries_new, axis=0)

    result_ref[0] = query_t[...].T * scale


def attend_backward_wrap(tile, query_ref, key_ref, value_ref, query_item_ref, key_item_ref, grad_ref, out_ref, lse_ref,
                         final_ref, sums_ref, result, key_wide, key_t, query_t):
    attend_backward_body(tile, query_ref, key_ref, value_ref, query_item_ref, key_item_ref, grad_ref, out_ref, lse_ref,
                         result, key_wide, key_t, query_t)
    final_ref[...] = result[...].astype(BF16)
    for k in range(3):
        sums_ref[k] = jnp.sum(result[k].reshape(-1, 8, result.shape[2]), axis=0)


def attend_backward(projected, query_item, key_item, grad, out, lse):
    tokens = projected.shape[0]
    width = projected.shape[1] // 3
    pair = 2 * HDIM
    pairs = width // pair
    block = lambda k: pl.BlockSpec((tokens, pair), lambda i: (0, i + k * pairs))
    fixed = pl.BlockSpec((tokens, 128), lambda i: (0, 0))
    return pl.pallas_call(
        functools.partial(attend_backward_wrap, 256),
        grid=(pairs,),
        in_specs=[block(0), block(1), block(2), fixed, fixed, block(0), block(0), pl.BlockSpec((1, 8, tokens), lambda i: (i, 0, 0))],
        out_specs=[pl.BlockSpec((3, tokens, pair), lambda i: (0, 0, i)), pl.BlockSpec((3, 8, pair), lambda i: (0, 0, i))],
        out_shape=[jax.ShapeDtypeStruct((3, tokens, width), BF16), jax.ShapeDtypeStruct((3, 8, width), F32)],
        scratch_shapes=[pltpu.VMEM((3, tokens, pair), F32), pltpu.VMEM((tokens, 2 * pair), BF16), pltpu.VMEM((pair, tokens), BF16), pltpu.VMEM((pair, tokens), F32)],
        compiler_params=pltpu.CompilerParams(vmem_limit_bytes=48 << 20, dimension_semantics=("arbitrary",)),
        cost_estimate=pl.CostEstimate(flops=20 * tokens * tokens * width, bytes_accessed=12 << 20, transcendentals=tokens * tokens * width // HDIM),
        name="attend_backward",
    )(projected, projected, projected, query_item, key_item, grad, out, lse)


def to_units(cells):
    canvases, rows, two, half, width = cells.shape
    shaped = cells.reshape(canvases, rows // 2, 2, two, half, width)
    return shaped.transpose(0, 2, 3, 1, 4, 5).reshape(canvases * 4, rows // 2, half, width)


def from_units(blocks, canvases):
    units, count, half, width = blocks.shape
    shaped = blocks.reshape(canvases, 2, 2, count, half, width)
    return shaped.transpose(0, 3, 1, 2, 4, 5).reshape(canvases, 2 * count, 2, half, width)


def unit_to_rows(values, half, rows, canvases):
    width = values.shape[-1]
    own = rows // 2
    padded = jnp.pad(values.reshape(half, half, width), ((1, 1), (0, 0), (0, 0)))
    blocks = jnp.stack(
        [padded[own * k : own * k + own + 2] for k in range(half // own)]
    )
    return from_units(exchange(blocks, "fsdp"), canvases)


def rows_to_unit(cells):
    blocks = exchange(to_units(cells), "fsdp")
    return blocks.reshape(-1, cells.shape[-1])


def per_device(
    tokens,
    cotangent,
    size_tags,
    step_ids,
    ada_weight,
    ada_bias,
    attn_kernel,
    attn_shift,
    qkv_weight,
    qv_bias,
    out_weight,
    out_bias,
    up_weight,
    up_bias,
    ffn_kernel,
    ffn_shift,
    down_weight,
    down_bias,
):
    canvases, rows, grid, width = tokens.shape[1:]
    half = grid // 2
    n_dp, n_fsdp = lax.axis_size("dp"), lax.axis_size("fsdp")
    count = n_dp * n_fsdp
    assert canvases * 4 == n_fsdp and rows * n_fsdp == grid
    fsdp_index = lax.axis_index("fsdp")
    every_bit = bits_of("fsdp") + bits_of("dp")
    hidden_units = up_weight.shape[1]
    shard = width // count
    ff_shard = hidden_units // count

    first_pair = lax.all_gather(
        jnp.concatenate([qkv_weight, out_weight], axis=1), EVERY, axis=0, tiled=True
    )
    qkv_full, out_full = first_pair[:, : 3 * width], first_pair[:, 3 * width :]
    up_rows = up_weight.reshape(shard, ff_shard * count // width, width).transpose(1, 0, 2)
    up_rows = up_rows.reshape(ff_shard, width)
    second_pair = lax.all_gather(
        jnp.concatenate([up_rows, down_weight], axis=0)[None], EVERY, axis=0, tiled=True
    )
    up_full = second_pair[:, :ff_shard].reshape(count, ff_shard // shard, shard, width)
    up_full = up_full.transpose(0, 2, 1, 3).reshape(width, hidden_units)
    down_full = second_pair[:, ff_shard:].reshape(hidden_units, width)

    parts = [
        ada_bias,
        attn_kernel,
        attn_shift,
        qv_bias,
        out_bias,
        up_bias,
        ffn_kernel,
        ffn_shift,
        down_bias,
        size_tags,
        step_ids,
    ]
    packed = gather_small(
        jnp.concatenate([part.astype(F32).reshape(-1) for part in parts]), every_bit
    )
    pieces = []
    start = 0
    for part in parts:
        size = math.prod(part.shape)
        pieces.append(packed[:, start : start + size])
        start += size
    whole = [
        piece.reshape((count,) + part.shape).swapaxes(0, 1).reshape(part.shape[0], -1)
        if part.ndim == 2
        else piece.reshape(-1)
        for piece, part in zip(pieces[:9], parts[:9])
    ]
    (
        ada_bias_full,
        attn_kernel_full,
        attn_shift_full,
        qv_bias_full,
        out_bias_full,
        up_bias_full,
        ffn_kernel_full,
        ffn_shift_full,
        down_bias_full,
    ) = whole
    tags = pieces[9].reshape(n_dp, n_fsdp, canvases)[:, 0].reshape(n_dp * canvases)
    steps = pieces[10].reshape(n_dp, n_fsdp, canvases, 4)[:, 0].reshape(n_dp * canvases, 4)

    chosen = jnp.where(tags[:, None] == 1, steps[:, :1], steps).reshape(-1)
    device = lax.axis_index("dp") * n_fsdp + fsdp_index
    feature = device * shard + jnp.arange(shard)
    half_width = width // 2
    frequency = jnp.exp(
        -math.log(10000.0) * (feature % half_width).astype(F32) / half_width
    )
    angles = chosen[:, None] * frequency
    embedded = jnp.where(feature < half_width, jnp.cos(angles), jnp.sin(angles))
    embedded = jax.nn.silu(embedded).astype(BF16)
    modulation = matmul(embedded, ada_weight)
    for axis, bit in bits_of("fsdp"):
        keep, give = halves(modulation, my_bit(axis, bit), 1)
        modulation = keep + swap(give, axis, bit)
    for axis, bit in bits_of("dp")[::-1]:
        keep, give = halves(modulation, my_bit(axis, bit), 0)
        modulation = keep + swap(give, axis, bit)
    for axis, bit in bits_of("fsdp")[::-1]:
        modulation = by_bit(
            modulation, swap(modulation, axis, bit), my_bit(axis, bit), 1, jnp.concatenate
        )
    modulation = (modulation + ada_bias_full).reshape(canvases, 4, 6 * width)
    first_row = fsdp_index * rows
    row_half = (first_row >= half).astype(jnp.int32)
    local_mod = lax.dynamic_slice_in_dim(modulation, 2 * row_half, 2, axis=1)
    shift_one, scale_one, gate_one, shift_two, scale_two, gate_two = [
        spread_items(local_mod[:, :, k * width : (k + 1) * width], grid) for k in range(6)
    ]

    big_item = size_tags[0] == 1
    big = big_item.astype(F32)
    edge = jnp.concatenate(
        [tokens[0][:, -2:], cotangent[0][:, -1:]], axis=1
    ), jnp.concatenate([tokens[0][:, :2], cotangent[0][:, :1]], axis=1)
    ends = n_fsdp - 1
    above = lax.ppermute(edge[0], "fsdp", [(i, i + 1) for i in range(ends)])
    below = lax.ppermute(edge[1], "fsdp", [(i + 1, i) for i in range(ends)])
    inputs = split_cols(jnp.concatenate([above[:, :2], tokens[0], below[:, :2]], axis=1))
    grad_out = split_cols(jnp.concatenate([above[:, 2:], cotangent[0], below[:, 2:]], axis=1))
    inputs = inputs.astype(F32)
    grad_out = grad_out.astype(F32)
    crosses_top = jnp.logical_and(first_row == half, jnp.logical_not(big_item))
    crosses_end = jnp.logical_and(first_row + rows == half, jnp.logical_not(big_item))
    top_ok = jnp.where(jnp.logical_or(fsdp_index == 0, crosses_top), 0.0, 1.0)
    end_ok = jnp.where(jnp.logical_or(fsdp_index == n_fsdp - 1, crosses_end), 0.0, 1.0)

    def keep_item(cells, extra):
        spot = jnp.arange(cells.shape[1])[None, :]
        flag = jnp.where(spot < extra, top_ok[:, None], 1.0)
        flag = jnp.where(spot >= cells.shape[1] - extra, end_ok[:, None], flag)
        return jnp.where(flag[:, :, None, None, None] > 0, cells, jnp.zeros_like(cells))

    normed_one, rate_one = layer_norm(inputs[:, 1:-1])
    first = keep_item((normed_one * (1.0 + scale_one) + shift_one).astype(BF16), 1)
    mixed = (conv(first, attn_kernel_full, big) + attn_shift_full).astype(BF16)
    mixed_unit = rows_to_unit(mixed)
    bias_row = jnp.concatenate([qv_bias_full[0], jnp.zeros((width,), F32), qv_bias_full[1]])
    projected = (matmul(mixed_unit, qkv_full) + bias_row).astype(BF16)
    unit_canvas = fsdp_index // 4
    unit_big = jnp.take(big_item, unit_canvas)
    side = (jnp.arange(half) >= half // 2).astype(jnp.int32)
    quad = (2 * side[:, None] + side[None, :]).reshape(-1)
    lane = jnp.arange(128)[None]
    hot = quad[:, None] == lane
    query_item = hot.astype(BF16)
    open_keys = jnp.logical_or(unit_big, jnp.logical_or(hot, lane >= 4))
    key_item = jnp.where(open_keys, 0.0, -1e30).astype(BF16)
    attended_unit, lse = attend_forward(projected, query_item, key_item)
    attended = unit_to_rows(attended_unit, half, rows, canvases)
    flat = attended.reshape(-1, width)
    branch_one = (matmul(flat, out_full) + out_bias_full).reshape(attended.shape)
    hidden = inputs + gate_one * branch_one
    normed_two, rate_two = layer_norm(hidden)
    second = (normed_two * (1.0 + scale_two) + shift_two).astype(BF16)

    own_shape = (canvases, rows, 2, half, width)
    grad_two_ext = (gate_two * grad_out).astype(BF16)
    grad_branch_two = grad_two_ext[:, 1:-1].reshape(-1, width)
    flags = jnp.stack([big, top_ok, end_ok], axis=1)
    branch_two, grad_second, grad_up, grad_down, ff_sums = feed_forward(
        flags,
        second.reshape(-1, width),
        grad_two_ext.reshape(-1, width),
        up_full,
        up_bias_full,
        ffn_kernel_full,
        ffn_shift_full,
        down_full,
        canvases,
        rows,
        half,
    )
    branch_two = (branch_two + down_bias_full).reshape(own_shape)
    grad_second = grad_second.reshape(own_shape)
    grad_ffn_kernel, grad_ffn_shift, grad_up_bias = ff_sums[:9], ff_sums[9], ff_sums[10]
    grad_up_rows = grad_up.astype(BF16).reshape(count, shard, ff_shard // shard, width)
    grad_up_rows = grad_up_rows.transpose(0, 2, 1, 3).reshape(count, ff_shard, width)
    ff_grads = jnp.concatenate(
        [grad_up_rows, grad_down.astype(BF16).reshape(count, ff_shard, width)], axis=1
    )
    ff_grads = lax.psum_scatter(ff_grads, EVERY, scatter_dimension=0, tiled=True)[0]
    grad_up = ff_grads[:ff_shard].reshape(ff_shard // shard, shard, width)
    grad_up = grad_up.transpose(1, 0, 2).reshape(shard, hidden_units).astype(F32)
    grad_down = ff_grads[ff_shard:].astype(F32)

    grad_own = grad_out[:, 1:-1]
    hidden_own = hidden[:, 2:-2]
    normed_two_own = normed_two[:, 2:-2]
    branch_one_own = branch_one[:, 2:-2]
    result = join_cols((hidden_own + gate_two * branch_two).astype(BF16))[None]
    grad_gate_two = item_sums(grad_own * branch_two)
    grad_down_bias = jnp.sum(grad_branch_two.astype(F32), axis=0)
    grad_scale_two = item_sums(grad_second * normed_two_own)
    grad_shift_two = item_sums(grad_second)
    grad_hidden = grad_own + layer_norm_back(
        grad_second * (1.0 + scale_two), normed_two_own, rate_two[:, 2:-2]
    )
    grad_gate_one = item_sums(grad_hidden * branch_one_own)
    grad_branch_one = (gate_one * grad_hidden).astype(BF16)
    flat_grad = grad_branch_one.reshape(-1, width)
    grad_out_bias = jnp.sum(flat_grad.astype(F32), axis=0)
    grad_attended = contract_cols(flat_grad, out_full).astype(BF16).reshape(own_shape)
    grad_unit = rows_to_unit(grad_attended)
    grad_out_weight = contract_rows(attended[:, 2:-2].reshape(-1, width), flat_grad)

    grad_parts, part_sums = attend_backward(
        projected, query_item, key_item, grad_unit, attended_unit, lse
    )
    grad_qkv = jnp.concatenate([contract_rows(mixed_unit, grad_parts[k]) for k in range(3)], axis=1)
    grad_qv_bias = jnp.stack([jnp.sum(part_sums[0], axis=0), jnp.sum(part_sums[2], axis=0)])
    grad_mixed_unit = sum(
        contract_cols(grad_parts[k], qkv_full[:, k * width : (k + 1) * width]) for k in range(3)
    ).astype(BF16)
    attn_grads = jnp.concatenate([grad_qkv, grad_out_weight], axis=1).astype(BF16)
    attn_grads = lax.psum_scatter(attn_grads, EVERY, scatter_dimension=0, tiled=True)
    grad_qkv = attn_grads[:, : 3 * width].astype(F32)
    grad_out_weight = attn_grads[:, 3 * width :].astype(F32)

    grad_mixed = unit_to_rows(grad_mixed_unit, half, rows, canvases)[:, 1:-1]
    grad_mixed = keep_item(grad_mixed, 1)
    own_mixed = grad_mixed[:, 1:-1].astype(F32)
    grad_attn_shift = jnp.sum(own_mixed, axis=(0, 1, 2, 3))
    grad_attn_kernel = tap_grads(first, own_mixed, big)
    grad_first = conv(grad_mixed, attn_kernel_full[::-1], big)
    normed_own = normed_one[:, 1:-1]
    grad_scale_one = item_sums(grad_first * normed_own)
    grad_shift_one = item_sums(grad_first)
    grad_inputs = grad_hidden + layer_norm_back(
        grad_first * (1.0 + scale_one), normed_own, rate_one[:, 1:-1]
    )
    grad_tokens = join_cols(grad_inputs.astype(BF16))[None]

    local_grad = jnp.concatenate(
        [
            grad_shift_one,
            grad_scale_one,
            grad_gate_one,
            grad_shift_two,
            grad_scale_two,
            grad_gate_two,
        ],
        axis=-1,
    )
    fsdp_bits = bits_of("fsdp")
    for axis, bit in fsdp_bits[:-1]:
        local_grad = local_grad + swap(local_grad, axis, bit)
    mod_grads = gather_small(local_grad, fsdp_bits[-1:] + bits_of("dp"))
    mod_grads = mod_grads.reshape(n_dp, 2, canvases, 2, 6 * width).transpose(0, 2, 1, 3, 4)
    mod_grads = mod_grads.reshape(n_dp * canvases * 4, 6 * width)
    grad_ada = jnp.dot(embedded.astype(F32).T, mod_grads, precision=lax.Precision.HIGHEST)
    bias_size = ada_bias.shape[0]
    grad_ada_bias = lax.dynamic_slice_in_dim(
        jnp.sum(mod_grads, axis=0), device * bias_size, bias_size
    )

    smalls = [
        grad_attn_kernel,
        grad_attn_shift,
        grad_qv_bias,
        grad_out_bias,
        grad_up_bias,
        grad_ffn_kernel,
        grad_ffn_shift,
        grad_down_bias,
    ]
    blocks = []
    for small in smalls:
        if small.ndim == 1:
            blocks.append(small.reshape(count, -1))
        else:
            lead = small.shape[0]
            blocks.append(small.reshape(lead, count, -1).swapaxes(0, 1).reshape(count, -1))
    summed = scatter_small(jnp.concatenate(blocks, axis=1), every_bit)[0]
    small_grads = []
    start = 0
    for small in smalls:
        size = math.prod(small.shape) // count
        piece = summed[start : start + size]
        small_grads.append(piece if small.ndim == 1 else piece.reshape(small.shape[0], -1))
        start += size
    (
        grad_attn_kernel,
        grad_attn_shift,
        grad_qv_bias,
        grad_out_bias,
        grad_up_bias,
        grad_ffn_kernel,
        grad_ffn_shift,
        grad_down_bias,
    ) = small_grads
    return (
        result,
        grad_tokens,
        grad_ada,
        grad_ada_bias,
        grad_attn_kernel,
        grad_attn_shift,
        grad_qkv,
        grad_qv_bias,
        grad_out_weight,
        grad_out_bias,
        grad_up,
        grad_up_bias,
        grad_ffn_kernel,
        grad_ffn_shift,
        grad_down,
        grad_down_bias,
    )


def solution(mesh):
    cells = P("dp", None, "fsdp", None, None)
    by_row = P(EVERY, None)
    by_col = P(None, EVERY)
    flat = P(EVERY)
    weights = (by_row, flat, by_col, flat, by_row, by_col, by_row, flat, by_row, flat, by_col, flat, by_row, flat)
    return jax.shard_map(
        per_device,
        mesh=mesh,
        in_specs=(cells, cells, P("dp", None), P("dp", None, None)) + weights,
        out_specs=(cells, cells) + weights,
        check_vma=False,
    )
```

```python
import functools
import math

import jax
import jax.numpy as jnp
from jax import lax
from jax.experimental import pallas as pl
from jax.experimental.pallas import tpu as pltpu
from jax.sharding import PartitionSpec as P

HEADS = 12
HDIM = 64
EVERY = ("dp", "fsdp")
F32 = jnp.float32
BF16 = jnp.bfloat16


def bits_of(axis):
    size = lax.axis_size(axis)
    count = size.bit_length() - 1
    assert 1 << count == size, axis
    return [(axis, 1 << k) for k in range(count)]


def my_bit(axis, bit):
    return (lax.axis_index(axis) // bit) % 2


def swap(value, axis, bit):
    size = lax.axis_size(axis)
    return lax.ppermute(value, axis, [(i, i ^ bit) for i in range(size)])


def by_bit(mine, other, flag, dim, join=jnp.stack):
    low = jnp.where(flag == 0, mine, other)
    high = jnp.where(flag == 0, other, mine)
    return join([low, high], axis=dim)


def halves(value, flag, dim):
    half = value.shape[dim] // 2
    keep = lax.dynamic_slice_in_dim(value, flag * half, half, axis=dim)
    give = lax.dynamic_slice_in_dim(value, (1 - flag) * half, half, axis=dim)
    return keep, give


def gather_small(value, bits):
    order = bits[::-1]
    for step, (axis, bit) in enumerate(order):
        value = by_bit(value, swap(value, axis, bit), my_bit(axis, bit), step)
    return value.reshape((1 << len(order),) + value.shape[len(order):])


def scatter_small(value, bits):
    sizes = [2] * len(bits)
    value = value.reshape(sizes + [value.shape[0] >> len(bits)] + list(value.shape[1:]))
    for step, (axis, bit) in enumerate(bits):
        dim = len(bits) - 1 - step
        flag = my_bit(axis, bit)
        keep, give = halves(value, flag, dim)
        value = keep + swap(give, axis, bit)
    return value.reshape(value.shape[len(bits):])


def contract_rows(left_side, right_side):
    return lax.dot_general(
        left_side, right_side, (((0,), (0,)), ((), ())), preferred_element_type=F32
    )


def contract_cols(left_side, right_side):
    return lax.dot_general(
        left_side, right_side, (((1,), (1,)), ((), ())), preferred_element_type=F32
    )


def matmul(left_side, right_side):
    return jnp.dot(left_side, right_side, preferred_element_type=F32)


GELU_C = math.sqrt(2.0 / math.pi)
GELU_A = 0.044715


def shifted(values, mask, step):
    lead = values.shape[0] * 8
    flat = values.reshape(lead, values.shape[2])
    return pltpu.roll(flat, step % lead, axis=0).reshape(values.shape) * mask


def conv_row(load, taps):
    even_sum = odd_sum = None
    for down in range(3):
        even, odd, odd_down, even_up = load(down)
        left, centre, right = taps[3 * down : 3 * down + 3]
        even_part = left * odd_down + centre * even + right * odd
        odd_part = left * even + centre * odd + right * even_up
        even_sum = even_part if even_sum is None else even_sum + even_part
        odd_sum = odd_part if odd_sum is None else odd_sum + odd_part
    return even_sum, odd_sum


def ffn_body(canvases, rows, half, lanes, flag_ref, second_ref, grad_ref, up_block, up_bias_ref, kernel_ref, shift_ref,
             down_block, branch_ref, grad_second_ref, grad_up_block, grad_down_block, sums_ref,
             cells, cells_side, grads, grads_side, active, grad_cells, second_t, up_ref, down_ref, grad_down_ref):
    step = pl.program_id(0)
    width = second_ref.shape[1]
    block = up_ref.shape[1]
    shard, ff_shard = up_block.shape[1], down_block.shape[1]
    for k in range(up_block.shape[0]):
        up_ref[k * shard : (k + 1) * shard, :] = up_block[k]
    for k in range(down_block.shape[0]):
        down_ref[k * ff_shard : (k + 1) * ff_shard, :] = down_block[k]
    grid = 2 * half
    group = half // 8
    tile = 256
    ext = rows + 4
    mid = rows + 2
    own = rows * grid

    @pl.when(step == 0)
    def _():
        branch_ref[...] = jnp.zeros_like(branch_ref)
        grad_second_ref[...] = jnp.zeros_like(grad_second_ref)
        for c in range(canvases):
            start = (c * ext + 2) * grid
            second_t[:, c * own : (c + 1) * own] = second_ref[start : start + own, :].T

    spot = lax.broadcasted_iota(jnp.int32, (group, 8, lanes), 0) * 8 + lax.broadcasted_iota(jnp.int32, (group, 8, lanes), 1)

    def masks(c):
        big = flag_ref[c, 0]
        down_mask = jnp.where(spot == 0, 0.0, jnp.where(spot == half // 2, big, 1.0))
        up_mask = jnp.where(spot == half - 1, 0.0, jnp.where(spot == half // 2 - 1, big, 1.0))
        return down_mask, up_mask

    @pl.loop(0, block // tile)
    def _(n):
        cols = pl.ds(pl.multiple_of(n * tile, tile), tile)
        product = matmul(second_ref[...], up_ref[:, cols]) + up_bias_ref[:, cols]
        cells[:, :, cols] = product.reshape(-1, 8, tile)
        weight = down_ref[pl.ds(pl.multiple_of(n * tile, tile), tile), :]
        grads[:, :, cols] = contract_cols(grad_ref[...], weight).reshape(-1, 8, tile)

    for c in range(canvases):
        @pl.when(flag_ref[c, 1] == 0)
        def _():
            cells[pl.ds(c * ext * grid // 8, 2 * grid // 8)] = jnp.zeros((2 * grid // 8, 8, block), F32)

        @pl.when(flag_ref[c, 2] == 0)
        def _():
            cells[pl.ds(((c + 1) * ext - 2) * grid // 8, 2 * grid // 8)] = jnp.zeros((2 * grid // 8, 8, block), F32)

    chunks = block // lanes
    per_row = grid // 8

    for c in range(canvases):
        down_mask, up_mask = masks(c)

        @pl.loop(0, ext)
        def _(r):
            base = (c * ext + r) * per_row
            for k in range(chunks):
                cols = slice(k * lanes, (k + 1) * lanes)
                even = cells[pl.ds(base, group), :, cols]
                odd = cells[pl.ds(base + group, group), :, cols]
                cells_side[pl.ds(base, group), :, cols] = shifted(odd, down_mask, 1)
                cells_side[pl.ds(base + group, group), :, cols] = shifted(even, up_mask, -1)

        @pl.loop(0, chunks)
        def _(k):
            cols = pl.ds(pl.multiple_of(k * lanes, lanes), lanes)
            taps = [kernel_ref[pl.ds(t, 1), cols][None] for t in range(9)]
            taps = [jnp.broadcast_to(t, (1, 8, lanes)) for t in taps]
            shift = jnp.broadcast_to(shift_ref[:, cols][None], (1, 8, lanes))

            @pl.loop(0, mid)
            def _(r):
                def load(down):
                    base = (c * ext + r + down) * per_row
                    return (cells[pl.ds(base, group), :, cols], cells[pl.ds(base + group, group), :, cols],
                            cells_side[pl.ds(base, group), :, cols], cells_side[pl.ds(base + group, group), :, cols])

                sums = conv_row(load, taps)
                here = (c * mid + r) * per_row
                outs = []
                for side in range(2):
                    v = sums[side] + shift
                    square = v * v
                    t = jnp.tanh(v * (GELU_C + (GELU_C * GELU_A) * square))
                    gate = 0.5 + 0.5 * t
                    slope = gate + (v * (2 * GELU_C + (6 * GELU_C * GELU_A) * square)) * (gate - gate * gate)
                    spots = pl.ds(here + side * group, group)
                    active[spots, :, cols] = (v * gate).astype(BF16)
                    outs.append(grads[spots, :, cols] * slope)
                    grads[spots, :, cols] = outs[-1]
                grads_side[pl.ds(here, group), :, cols] = shifted(outs[1], down_mask, 1)
                grads_side[pl.ds(here + group, group), :, cols] = shifted(outs[0], up_mask, -1)

        for row, flag in ((0, 1), (mid - 1, 2)):
            @pl.when(flag_ref[c, flag] == 0)
            def _():
                spots = pl.ds((c * mid + row) * per_row, per_row)
                grads[spots] = jnp.zeros((per_row, 8, block), F32)
                grads_side[spots] = jnp.zeros((per_row, 8, block), F32)

        @pl.loop(0, chunks)
        def _(k):
            cols = pl.ds(pl.multiple_of(k * lanes, lanes), lanes)
            taps = [kernel_ref[pl.ds(8 - t, 1), cols][None] for t in range(9)]
            taps = [jnp.broadcast_to(t, (1, 8, lanes)) for t in taps]

            def row_step(r, sums):
                def load_grads(down):
                    base = (c * mid + r + down) * per_row
                    return (grads[pl.ds(base, group), :, cols], grads[pl.ds(base + group, group), :, cols],
                            grads_side[pl.ds(base, group), :, cols], grads_side[pl.ds(base + group, group), :, cols])

                back_even, back_odd = conv_row(load_grads, taps)
                here = (c * rows + r) * per_row
                grad_cells[pl.ds(here, group), :, cols] = back_even.astype(BF16)
                grad_cells[pl.ds(here + group, group), :, cols] = back_odd.astype(BF16)
                mine = (c * mid + r + 1) * per_row
                g_even = grads[pl.ds(mine, group), :, cols]
                g_odd = grads[pl.ds(mine + group, group), :, cols]
                new = []
                for down in range(3):
                    base = (c * ext + r + 1 + down) * per_row
                    even = cells[pl.ds(base, group), :, cols]
                    odd = cells[pl.ds(base + group, group), :, cols]
                    odd_down = cells_side[pl.ds(base, group), :, cols]
                    even_up = cells_side[pl.ds(base + group, group), :, cols]
                    for for_even, for_odd in ((odd_down, even), (even, odd), (odd, even_up)):
                        new.append(jnp.sum(for_even * g_even + for_odd * g_odd, axis=0))
                new.append(jnp.sum(g_even + g_odd, axis=0))
                new.append(jnp.sum(back_even + back_odd, axis=0))
                return tuple(s + v for s, v in zip(sums, new))

            zero = jnp.zeros((8, lanes), F32)
            sums = lax.fori_loop(0, rows, row_step, (zero,) * 11)
            for t in range(11):
                total = jnp.sum(sums[t], axis=0, keepdims=True)
                if c == 0:
                    sums_ref[pl.ds(t, 1), cols] = total
                else:
                    sums_ref[pl.ds(t, 1), cols] += total

    for c in range(canvases):
        mine = slice(c * own, (c + 1) * own)
        act_rows = pl.ds((c * mid + 1) * per_row, rows * per_row)
        own_grad = grad_ref[(c * mid + 1) * grid : (c * mid + 1) * grid + own, :]

        @pl.loop(0, width // tile)
        def _(n):
            cols = pl.ds(pl.multiple_of(n * tile, tile), tile)
            branch_ref[mine, cols] += matmul(active[act_rows].reshape(own, block), down_ref[:, cols])
            weight = up_ref[pl.ds(pl.multiple_of(n * tile, tile), tile), :]
            spots = pl.ds(c * rows * per_row, rows * per_row)
            grad_second_ref[mine, cols] += contract_cols(grad_cells[spots].reshape(own, block), weight)

        @pl.loop(0, block // tile)
        def _(n):
            cols = pl.ds(pl.multiple_of(n * tile, tile), tile)
            part = contract_rows(active[act_rows, :, cols].reshape(own, tile), own_grad)
            if c == 0:
                grad_down_ref[cols, :] = part
            else:
                grad_down_ref[cols, :] += part

    @pl.loop(0, block // tile)
    def _(n):
        cols = pl.ds(pl.multiple_of(n * tile, tile), tile)
        part = matmul(second_t[...], grad_cells[:, :, cols].reshape(-1, tile))
        grad_up_block[:, :, cols] = part.reshape(-1, shard, tile).astype(BF16)

    for k in range(down_block.shape[0]):
        grad_down_block[k] = grad_down_ref[k * ff_shard : (k + 1) * ff_shard, :].astype(BF16)


def feed_forward(flags, second, grad_two, pair, up_bias, kernel, shift, canvases, rows, half):
    count, both, width = pair.shape
    ff_shard = both // 2
    shard, hidden = width // count, ff_shard * count
    block, lanes = width, 128
    per_block = block // ff_shard
    grid = 2 * half
    ext, mid, own = [canvases * n * grid for n in (rows + 4, rows + 2, rows)]
    kernel = jnp.pad(kernel, ((0, 7), (0, 0)))
    fixed = lambda shape: pl.BlockSpec(shape, lambda i: (0, 0), pipeline_mode=pl.Buffered(1))
    cols = lambda n: pl.BlockSpec((n, block), lambda i: (0, i))
    if shard % 8 == 0:
        up, down = pair, pair
        up_spec = pl.BlockSpec((count, shard, block), lambda i: (0, i, 0))
        down_spec = pl.BlockSpec((per_block, ff_shard, width), lambda i: (i, 1, 0))
        grad_spec = up_spec
        grad_shape = (count, ff_shard, width)
    else:
        up = pair[:, :ff_shard].reshape(count, ff_shard // shard, shard, width).swapaxes(0, 1)
        up, down = up.reshape(-1, width, width), pair[:, ff_shard:]
        up_spec = pl.BlockSpec((1, width, block), lambda i: (i, 0, 0))
        down_spec = pl.BlockSpec((per_block, ff_shard, width), lambda i: (i, 0, 0))
        grad_spec = up_spec
        grad_shape = (hidden // block, width, width)
    outs = pl.pallas_call(
        functools.partial(ffn_body, canvases, rows, half, lanes),
        grid=(hidden // block,),
        in_specs=[
            pl.BlockSpec(memory_space=pltpu.SMEM),
            fixed((ext, width)),
            fixed((mid, width)),
            up_spec,
            cols(1),
            cols(16),
            cols(1),
            down_spec,
        ],
        out_specs=[
            pl.BlockSpec((own, width), lambda i: (0, 0)),
            pl.BlockSpec((own, width), lambda i: (0, 0)),
            grad_spec,
            pl.BlockSpec((per_block, ff_shard, width), lambda i: (i, 0, 0)),
            cols(16),
        ],
        out_shape=[
            jax.ShapeDtypeStruct((own, width), F32),
            jax.ShapeDtypeStruct((own, width), F32),
            jax.ShapeDtypeStruct(grad_shape, BF16),
            jax.ShapeDtypeStruct((count, ff_shard, width), BF16),
            jax.ShapeDtypeStruct((16, hidden), F32),
        ],
        scratch_shapes=[
            pltpu.VMEM((ext // 8, 8, block), F32),
            pltpu.VMEM((ext // 8, 8, block), F32),
            pltpu.VMEM((mid // 8, 8, block), F32),
            pltpu.VMEM((mid // 8, 8, block), F32),
            pltpu.VMEM((mid // 8, 8, block), BF16),
            pltpu.VMEM((own // 8, 8, block), BF16),
            pltpu.VMEM((width, own), BF16),
            pltpu.VMEM((width, block), BF16),
            pltpu.VMEM((block, width), BF16),
            pltpu.VMEM((block, width), F32),
        ],
        compiler_params=pltpu.CompilerParams(vmem_limit_bytes=60 << 20, dimension_semantics=("arbitrary",)),
        cost_estimate=pl.CostEstimate(flops=12 * own * width * hidden, bytes_accessed=40 << 20, transcendentals=own * hidden),
        name="feed_forward",
    )(flags, second, grad_two, up, up_bias[None], kernel, shift[None], down)
    branch, grad_second, grad_up, grad_down, sums = outs
    if shard % 8:
        grad_up = grad_up.reshape(-1, count, shard, width).swapaxes(0, 1).reshape(count, ff_shard, width)
    return branch, grad_second, jnp.concatenate([grad_up, grad_down], axis=1), sums


def one_head(pair, head):
    lane = lax.broadcasted_iota(jnp.int32, pair.shape, 1)
    return jnp.where((lane < HDIM) == (head == 0), pair, jnp.zeros_like(pair))


def attend_forward_body(tile, count, half, place_ref, query_ref, key_ref, value_ref, query_item_ref, key_item_ref, spread_ref, lse_ref, key_wide, out_ref):
    tokens = query_ref.shape[0]
    pair = query_ref.shape[1]
    scale = HDIM ** -0.5
    key_wide[:, :pair] = key_ref[...]
    key_wide[:, pair:] = key_item_ref[...]

    @pl.loop(0, tokens // tile)
    def _(n):
        spots = pl.ds(pl.multiple_of(n * tile, tile), tile)
        query = query_ref[spots, :] * jnp.asarray(scale, BF16)
        outs = []
        for head in range(2):
            wide = jnp.concatenate([one_head(query, head), query_item_ref[spots, :]], axis=1)
            scores = contract_cols(wide, key_wide[...])
            top = jnp.max(scores, axis=1, keepdims=True)
            weights = jnp.exp(scores - top)
            total = jnp.sum(weights, axis=1, keepdims=True)
            outs.append(matmul(weights.astype(BF16), value_ref[...]) / total)
            lse = jnp.broadcast_to(top + jnp.log(total), (tile, 128))
            lse_ref[0, pl.ds(head, 1), spots] = lse.T[:1]
        lane = lax.broadcasted_iota(jnp.int32, outs[0].shape, 1)
        out_ref[spots, :] = jnp.where(lane < HDIM, outs[0], outs[1]).astype(BF16)

    spread_lines(spread_ref, out_ref[...], count, half, place_ref[0], slice(None))


def attend_forward(place, projected, query_item, key_item, count, half):
    tokens = projected.shape[0]
    width = projected.shape[1] // 3
    pair = 2 * HDIM
    pairs = width // pair
    lines = tokens // count + 2 * half
    block = lambda k: pl.BlockSpec((tokens, pair), lambda i: (0, i + k * pairs))
    fixed = pl.BlockSpec((tokens, 128), lambda i: (0, 0))
    return pl.pallas_call(
        functools.partial(attend_forward_body, 256, count, half),
        grid=(pairs,),
        in_specs=[pl.BlockSpec(memory_space=pltpu.SMEM), block(0), block(1), block(2), fixed, fixed],
        out_specs=[pl.BlockSpec((count, lines, pair), lambda i: (0, 0, i)), pl.BlockSpec((1, 8, tokens), lambda i: (i, 0, 0))],
        out_shape=[jax.ShapeDtypeStruct((count, lines, width), BF16), jax.ShapeDtypeStruct((pairs, 8, tokens), F32)],
        scratch_shapes=[pltpu.VMEM((tokens, 2 * pair), BF16), pltpu.VMEM((tokens, pair), BF16)],
        compiler_params=pltpu.CompilerParams(vmem_limit_bytes=40 << 20, dimension_semantics=("arbitrary",)),
        cost_estimate=pl.CostEstimate(flops=8 * tokens * tokens * width, bytes_accessed=8 << 20, transcendentals=tokens * tokens * width // HDIM),
        name="attend_forward",
    )(place, projected, projected, projected, query_item, key_item)


def attend_backward_body(tile, count, half, query_ref, key_ref, value_ref, query_item_ref, key_item_ref, spread_ref, lse_ref, *refs):
    blocks = refs[:count]
    final_ref, sums_ref, result_ref, key_wide, key_t, query_t, grad_ref, out_ref = refs[count:]
    tokens = query_ref.shape[0]
    pair = query_ref.shape[1]
    size = tokens // count
    scale = HDIM ** -0.5
    key_wide[:, :pair] = key_ref[...]
    key_wide[:, pair:] = key_item_ref[...]
    key_t[...] = key_ref[...].T
    for k in range(count):
        grad_ref[k * size : (k + 1) * size, :] = blocks[k][...]
        out_ref[k * size : (k + 1) * size, :] = spread_ref[k, half : half + size, :]

    result_ref[1] = jnp.zeros_like(result_ref[1])
    result_ref[2] = jnp.zeros_like(result_ref[2])

    @pl.loop(0, tokens // tile)
    def _(n):
        spots = pl.ds(pl.multiple_of(n * tile, tile), tile)
        query = query_ref[spots, :] * jnp.asarray(scale, BF16)
        grad = grad_ref[spots, :]
        both = (grad.astype(F32) * out_ref[spots, :].astype(F32)).T
        keys_new = []
        values_new = []
        queries_new = []
        for head in range(2):
            own = slice(head * HDIM, (head + 1) * HDIM)
            centre = jnp.sum(both[own], axis=0, keepdims=True)
            wide = jnp.concatenate([one_head(query, head), query_item_ref[spots, :]], axis=1)
            weights = jnp.exp(contract_cols(key_wide[...], wide) - lse_ref[0, pl.ds(head, 1), spots])
            grad_weights = contract_cols(value_ref[...], one_head(grad, head))
            grad_scores = (weights * (grad_weights - centre)).astype(BF16)
            values_new.append(matmul(weights.astype(BF16), grad))
            keys_new.append(matmul(grad_scores, query))
            queries_new.append(matmul(key_t[...], grad_scores)[own])
        lane = lax.broadcasted_iota(jnp.int32, keys_new[0].shape, 1)
        result_ref[1] += jnp.where(lane < HDIM, keys_new[0], keys_new[1])
        result_ref[2] += jnp.where(lane < HDIM, values_new[0], values_new[1])
        query_t[:, spots] = jnp.concatenate(queries_new, axis=0)

    result_ref[0] = query_t[...].T * scale
    final_ref[...] = result_ref[...].astype(BF16)
    for k in range(3):
        sums_ref[k] = jnp.sum(fold(result_ref[k]), axis=0)


def attend_backward(projected, query_item, key_item, blocks, spread, lse, half):
    tokens = projected.shape[0]
    width = projected.shape[1] // 3
    pair = 2 * HDIM
    pairs = width // pair
    count = len(blocks)
    lines = tokens // count + 2 * half
    block = lambda k: pl.BlockSpec((tokens, pair), lambda i: (0, i + k * pairs))
    fixed = pl.BlockSpec((tokens, 128), lambda i: (0, 0))
    return pl.pallas_call(
        functools.partial(attend_backward_body, 256, count, half),
        grid=(pairs,),
        in_specs=[block(0), block(1), block(2), fixed, fixed]
        + [pl.BlockSpec((count, lines, pair), lambda i: (0, 0, i)), pl.BlockSpec((1, 8, tokens), lambda i: (i, 0, 0))]
        + [pl.BlockSpec((tokens // count, pair), lambda i: (0, i))] * count,
        out_specs=[pl.BlockSpec((3, tokens, pair), lambda i: (0, 0, i)), pl.BlockSpec((3, 8, pair), lambda i: (0, 0, i))],
        out_shape=[jax.ShapeDtypeStruct((3, tokens, width), BF16), jax.ShapeDtypeStruct((3, 8, width), F32)],
        scratch_shapes=[pltpu.VMEM((3, tokens, pair), F32), pltpu.VMEM((tokens, 2 * pair), BF16), pltpu.VMEM((pair, tokens), BF16), pltpu.VMEM((pair, tokens), F32)] + [pltpu.VMEM((tokens, pair), BF16)] * 2,
        compiler_params=pltpu.CompilerParams(vmem_limit_bytes=48 << 20, dimension_semantics=("arbitrary",)),
        cost_estimate=pl.CostEstimate(flops=20 * tokens * tokens * width, bytes_accessed=12 << 20, transcendentals=tokens * tokens * width // HDIM),
        name="attend_backward",
    )(projected, projected, projected, query_item, key_item, spread, lse, *blocks)


def column_order(size, grid, back):
    here = lax.broadcasted_iota(jnp.int32, (size, size), 1 if back else 0)
    there = lax.broadcasted_iota(jnp.int32, (size, size), 0 if back else 1)
    spot = here % grid
    source = here - spot + 2 * (spot % (grid // 2)) + spot // (grid // 2)
    return (source == there).astype(BF16)


def rows_at(row, grid):
    return pl.ds(pl.multiple_of(row * grid, grid), grid)


def normalise(values):
    centre = values - jnp.mean(values, axis=-1, keepdims=True)
    rate = lax.rsqrt(jnp.mean(centre * centre, axis=-1, keepdims=True) + 1e-06)
    return centre * rate, rate


def normalise_back(grad, normed, rate):
    mean_grad = jnp.mean(grad, axis=-1, keepdims=True)
    mean_both = jnp.mean(grad * normed, axis=-1, keepdims=True)
    return rate * (grad - mean_grad - normed * mean_both)


def fold(values):
    return values.reshape(-1, 8, values.shape[-1])


def half_sums(values):
    parts = values.reshape(2, 2, -1, 8, values.shape[-1])
    return jnp.sum(parts, axis=(0, 2))


def edge_masks(flag_ref, c, half, lanes):
    shape = (half // 8, 8, lanes)
    spot = lax.broadcasted_iota(jnp.int32, shape, 0) * 8 + lax.broadcasted_iota(jnp.int32, shape, 1)
    big = flag_ref[c, 0]
    down_mask = jnp.where(spot == 0, 0.0, jnp.where(spot == half // 2, big, 1.0))
    up_mask = jnp.where(spot == half - 1, 0.0, jnp.where(spot == half // 2 - 1, big, 1.0))
    return down_mask, up_mask


def fill_sides(cells, side, down_mask, up_mask, base, chunks, lanes):
    group = down_mask.shape[0]
    for k in range(chunks):
        cols = slice(k * lanes, (k + 1) * lanes)
        even = cells[pl.ds(base, group), :, cols]
        odd = cells[pl.ds(base + group, group), :, cols]
        side[pl.ds(base, group), :, cols] = shifted(odd, down_mask, 1)
        side[pl.ds(base + group, group), :, cols] = shifted(even, up_mask, -1)


def load_row(cells, side, base, group, cols):
    return (
        cells[pl.ds(base, group), :, cols],
        cells[pl.ds(base + group, group), :, cols],
        side[pl.ds(base, group), :, cols],
        side[pl.ds(base + group, group), :, cols],
    )


def spread_tap(ref, row, cols, lanes):
    return jnp.broadcast_to(ref[pl.ds(row, 1), cols][None], (1, 8, lanes))


def whole_call(body, inputs, outputs, scratch, name, flops, limit=60, scalars=1):
    moved = sum(math.prod(v.shape) * v.dtype.itemsize for v in list(inputs) + list(outputs))
    vmem = pl.BlockSpec(memory_space=pltpu.VMEM)
    smem = pl.BlockSpec(memory_space=pltpu.SMEM)
    return pl.pallas_call(
        body,
        in_specs=[smem] * scalars + [vmem] * (len(inputs) - scalars),
        out_specs=[vmem] * len(outputs),
        out_shape=list(outputs),
        scratch_shapes=scratch,
        compiler_params=pltpu.CompilerParams(vmem_limit_bytes=limit << 20),
        cost_estimate=pl.CostEstimate(flops=flops, bytes_accessed=moved, transcendentals=0),
        name=name,
    )(*inputs)


def sorted_rows(source, dest, count, grid, back):
    size = 2 * grid
    order = column_order(size, grid, back)

    @pl.loop(0, count // 2)
    def _(n):
        spots = pl.ds(pl.multiple_of(n * size, size), size)
        dest[spots, :] = matmul(order, source[spots, :]).astype(BF16)


def prepare_body(canvases, rows, half, flag_ref, place_ref, inputs_ref, grad_ref, kernel_ref, sorted_ref, grad_sorted_ref, out_ref, cells, side):
    grid, lanes = 2 * half, 128
    width = inputs_ref.shape[1]
    group, per_row, chunks = half // 8, grid // 8, width // lanes
    ext, mid = rows + 4, rows + 2
    me = place_ref[0]
    sorted_rows(inputs_ref, sorted_ref, canvases * ext, grid, False)
    for c in range(canvases):
        down_mask, up_mask = edge_masks(flag_ref, c, half, lanes)

        @pl.loop(0, mid)
        def _(r):
            normed, _ = normalise(sorted_ref[rows_at(c * ext + r + 1, grid), :].astype(F32))
            keep = jnp.where(r == 0, flag_ref[c, 1], jnp.where(r == mid - 1, flag_ref[c, 2], 1.0))
            base = (c * mid + r) * per_row
            cells[pl.ds(base, per_row)] = fold(normed * keep)
            fill_sides(cells, side, down_mask, up_mask, base, chunks, lanes)

        @pl.loop(0, chunks)
        def _(k):
            cols = pl.ds(pl.multiple_of(k * lanes, lanes), lanes)
            taps = [spread_tap(kernel_ref, t, cols, lanes) for t in range(9)]

            @pl.loop(0, rows // 2)
            def _(i):
                spots = pl.ds(pl.multiple_of(i * half, half), half)
                for a in range(2):
                    load = lambda down: load_row(cells, side, (c * mid + 2 * i + a + down) * per_row, group, cols)
                    sums = conv_row(load, taps)
                    for b in range(2):
                        unit = jnp.bitwise_xor(c * 4 + a * 2 + b, me)
                        out_ref[unit, spots, cols] = sums[b].reshape(half, lanes).astype(BF16)

    sorted_rows(grad_ref, grad_sorted_ref, canvases * mid, grid, False)


def prepare(flags, place, inputs, grad_out, kernel, canvases, rows, half):
    width = inputs.shape[1]
    mid = canvases * (rows + 2) * half * 2
    return whole_call(
        functools.partial(prepare_body, canvases, rows, half),
        (flags, place, inputs, grad_out, kernel),
        (
            jax.ShapeDtypeStruct(inputs.shape, BF16),
            jax.ShapeDtypeStruct(grad_out.shape, BF16),
            jax.ShapeDtypeStruct((canvases * 4, rows // 2 * half, width), BF16),
        ),
        [pltpu.VMEM((mid // 8, 8, width), F32)] * 2,
        "prepare",
        30 * inputs.shape[0] * width,
        scalars=2,
    )


def project_body(count, half, place_ref, *refs):
    blocks, (scale_ref, add_ref, weight_ref, bias_ref, mixed_ref, out_ref) = refs[:count], refs[count:]
    me, odd_row = place_ref[0], place_ref[1]
    size = blocks[0].shape[0]
    lines = size // half

    @pl.when(pl.program_id(0) == 0)
    def _():
        for k in range(count):
            owner = jnp.bitwise_xor(k, me)
            side = owner // (count // 2)

            @pl.loop(0, lines)
            def _(i):
                at_edge = jnp.where(odd_row == 0, jnp.where(i == 0, place_ref[2 + owner], 0), jnp.where(i == lines - 1, place_ref[2 + count + owner], 0))
                spots = pl.ds(pl.multiple_of(i * half, half), half)
                value = blocks[k][spots, :].astype(F32) * scale_ref[side] + add_ref[at_edge * 2 + side]
                mixed_ref[pl.ds(pl.multiple_of(k * size + i * half, half), half), :] = value.astype(BF16)

    out_ref[...] = (matmul(mixed_ref[...], weight_ref[...]) + bias_ref[...]).astype(BF16)


def project(place, blocks, scale, add, weight, bias, half):
    count = len(blocks)
    size, width = blocks[0].shape
    tokens, tile = count * size, 256
    fixed = lambda value: pl.BlockSpec(value.shape, lambda i: (0,) * value.ndim, pipeline_mode=pl.Buffered(1))
    cols = lambda n: pl.BlockSpec((n, tile), lambda i: (0, i))
    return pl.pallas_call(
        functools.partial(project_body, count, half),
        grid=(3 * width // tile,),
        in_specs=[pl.BlockSpec(memory_space=pltpu.SMEM)] + [fixed(block) for block in blocks] + [fixed(scale), fixed(add), cols(width), cols(1)],
        out_specs=[pl.BlockSpec((tokens, width), lambda i: (0, 0)), cols(tokens)],
        out_shape=[jax.ShapeDtypeStruct((tokens, width), BF16), jax.ShapeDtypeStruct((tokens, 3 * width), BF16)],
        compiler_params=pltpu.CompilerParams(vmem_limit_bytes=40 << 20, dimension_semantics=("arbitrary",)),
        cost_estimate=pl.CostEstimate(flops=6 * tokens * width * width, bytes_accessed=12 << 20, transcendentals=0),
        name="project",
    )(place, *blocks, scale, add, weight, bias)


def middle_body(canvases, rows, half, count, flag_ref, place_ref, *refs):
    blocks = refs[:count]
    inputs_ref, weight_ref, bias_ref, mods_ref, second_ref, hidden_ref, branch_ref, attended_ref, wide, product = refs[count:]
    grid = 2 * half
    width = inputs_ref.shape[1]
    ext = rows + 4
    me = place_ref[0]
    lines = rows // 2 + 2
    tile = 256
    for k in range(count):
        unit = jnp.bitwise_xor(k, me)
        canvas, a, b = unit // 4, (unit // 2) % 2, unit % 2

        @pl.loop(0, lines)
        def _(i):
            start = (canvas * ext + 2 * i + a) * grid + b * half
            wide[pl.ds(pl.multiple_of(start, half), half), :] = blocks[k][pl.ds(pl.multiple_of(i * half, half), half), :]

    @pl.loop(0, width // tile)
    def _(n):
        cols = pl.ds(pl.multiple_of(n * tile, tile), tile)
        product[:, cols] = matmul(wide[...], weight_ref[:, cols]) + bias_ref[:, cols]

    for c in range(canvases):
        own = slice((c * ext + 2) * grid, (c * ext + 2 + rows) * grid)
        attended_ref[c * rows * grid : (c + 1) * rows * grid, :] = wide[own, :]

        def line(r):
            spots = rows_at(c * ext + r, grid)
            branch = product[spots, :]
            hidden = inputs_ref[spots, :].astype(F32) + mods_ref[c, 2] * branch
            normed, _ = normalise(hidden)
            second_ref[spots, :] = (normed * (1.0 + mods_ref[c, 4]) + mods_ref[c, 3]).astype(BF16)
            return branch, hidden

        for r in (0, 1, rows + 2, rows + 3):
            line(r)

        @pl.loop(0, rows)
        def _(r):
            branch, hidden = line(r + 2)
            spots = rows_at(c * rows + r, grid)
            branch_ref[spots, :] = branch
            hidden_ref[spots, :] = hidden


def middle(flags, place, blocks, inputs, weight, bias, mods, canvases, rows, half):
    width = inputs.shape[1]
    own = canvases * rows * 2 * half
    return whole_call(
        functools.partial(middle_body, canvases, rows, half, len(blocks)),
        (flags, place, *blocks, inputs, weight, bias, mods),
        (
            jax.ShapeDtypeStruct(inputs.shape, BF16),
            jax.ShapeDtypeStruct((own, width), F32),
            jax.ShapeDtypeStruct((own, width), F32),
            jax.ShapeDtypeStruct((own, width), BF16),
        ),
        [pltpu.VMEM(inputs.shape, BF16), pltpu.VMEM(inputs.shape, F32)],
        "middle",
        2 * inputs.shape[0] * width * width,
        scalars=2,
    )


def turn_body(canvases, rows, half, place_ref, branch_two_ref, grad_second_ref, hidden_ref, branch_ref, grad_out_ref, weight_ref, bias_ref,
              mods_ref, out_ref, grad_hidden_ref, grad_branch_ref, blocks_ref, half_ref, bias_sums_ref, result):
    grid = 2 * half
    width = hidden_ref.shape[1]
    me = place_ref[0]
    tile = 256
    half_ref[...] = jnp.zeros_like(half_ref)
    bias_sums_ref[...] = jnp.zeros_like(bias_sums_ref)
    for c in range(canvases):

        @pl.loop(0, rows)
        def _(r):
            spots = rows_at(c * rows + r, grid)
            grad_out = grad_out_ref[rows_at(c * (rows + 2) + r + 1, grid), :].astype(F32)
            branch_two = branch_two_ref[spots, :] + bias_ref[...]
            hidden = hidden_ref[spots, :]
            result[spots, :] = (hidden + mods_ref[c, 5] * branch_two).astype(BF16)
            normed, rate = normalise(hidden)
            grad = grad_second_ref[spots, :]
            grad_hidden = grad_out + normalise_back(grad * (1.0 + mods_ref[c, 4]), normed, rate)
            grad_hidden_ref[spots, :] = grad_hidden
            grad_branch = (mods_ref[c, 2] * grad_hidden).astype(BF16)
            grad_branch_ref[spots, :] = grad_branch
            half_ref[c, 0] += half_sums(grad_hidden * branch_ref[spots, :])
            half_ref[c, 1] += half_sums(grad)
            half_ref[c, 2] += half_sums(grad * normed)
            half_ref[c, 3] += half_sums(grad_out * branch_two)
            bias_sums_ref[0] += jnp.sum(fold(grad_branch.astype(F32)), axis=0)
            low = (mods_ref[c, 5] * grad_out).astype(BF16).astype(F32)
            bias_sums_ref[1] += jnp.sum(fold(low), axis=0)

    @pl.loop(0, width // tile)
    def _(n):
        cols = pl.ds(pl.multiple_of(n * tile, tile), tile)
        product = contract_cols(grad_branch_ref[...], weight_ref[cols, :]).astype(BF16)
        for c in range(canvases):
            for r in range(rows):
                for b in range(2):
                    unit = jnp.bitwise_xor(c * 4 + r % 2 * 2 + b, me)
                    start = (c * rows + r) * grid + b * half
                    line = r // 2 * half
                    blocks_ref[unit, line : line + half, cols] = product[start : start + half]

    sorted_rows(result, out_ref, canvases * rows, grid, True)


def turn(place, branch_two, grad_second, hidden, branch, grad_out, weight, bias, mods, canvases, rows, half):
    own, width = hidden.shape
    return whole_call(
        functools.partial(turn_body, canvases, rows, half),
        (place, branch_two, grad_second, hidden, branch, grad_out, weight, bias, mods),
        (
            jax.ShapeDtypeStruct((own, width), BF16),
            jax.ShapeDtypeStruct((own, width), F32),
            jax.ShapeDtypeStruct((own, width), BF16),
            jax.ShapeDtypeStruct((canvases * 4, rows // 2 * half, width), BF16),
            jax.ShapeDtypeStruct((canvases, 4, 2, 8, width), F32),
            jax.ShapeDtypeStruct((2, 8, width), F32),
        ),
        [pltpu.VMEM((own, width), BF16)],
        "turn",
        2 * own * width * width,
    )


def spread_lines(out_ref, value, count, half, me, cols):
    size = value.shape[0] // count
    for k in range(count):
        owner = jnp.bitwise_xor(k, me)
        block = value[k * size : (k + 1) * size]
        out_ref[k, half : half + size, cols] = block

        @pl.when(owner + 1 < count)
        def _():
            out_ref[jnp.bitwise_xor(owner + 1, me), :half, cols] = block[size - half :]

        @pl.when(owner > 0)
        def _():
            out_ref[jnp.bitwise_xor(owner - 1, me), half + size :, cols] = block[:half]

        @pl.when(owner == 0)
        def _():
            out_ref[k, :half, cols] = jnp.zeros_like(block[:half])

        @pl.when(owner + 1 == count)
        def _():
            out_ref[k, half + size :, cols] = jnp.zeros_like(block[:half])


def project_back_body(count, half, place_ref, parts_ref, weight_ref, out_ref):
    width = parts_ref.shape[2]
    total = contract_cols(parts_ref[0], weight_ref[:, :width])
    for k in (1, 2):
        total += contract_cols(parts_ref[k], weight_ref[:, k * width : (k + 1) * width])
    spread_lines(out_ref, total.astype(BF16), count, half, place_ref[0], slice(None))


def project_back(place, parts, weight, count, half):
    _, tokens, width = parts.shape
    tile = 256
    lines = tokens // count + 2 * half
    return pl.pallas_call(
        functools.partial(project_back_body, count, half),
        grid=(width // tile,),
        in_specs=[
            pl.BlockSpec(memory_space=pltpu.SMEM),
            pl.BlockSpec((3, tokens, width), lambda i: (0, 0, 0), pipeline_mode=pl.Buffered(1)),
            pl.BlockSpec((tile, 3 * width), lambda i: (i, 0)),
        ],
        out_specs=pl.BlockSpec((count, lines, tile), lambda i: (0, 0, i)),
        out_shape=jax.ShapeDtypeStruct((count, lines, width), BF16),
        compiler_params=pltpu.CompilerParams(vmem_limit_bytes=40 << 20, dimension_semantics=("arbitrary",)),
        cost_estimate=pl.CostEstimate(flops=6 * tokens * width * width, bytes_accessed=12 << 20, transcendentals=0),
        name="project_back",
    )(place, parts, weight)


def finish_body(canvases, rows, half, count, flag_ref, place_ref, *refs):
    blocks = refs[:count]
    inputs_ref, grad_hidden_ref, kernel_ref, mods_ref, out_ref, half_ref, sums_ref, cells, side, grads, grads_side, back, result = refs[count:]
    grid, lanes = 2 * half, 128
    width = inputs_ref.shape[1]
    group, per_row, chunks = half // 8, grid // 8, width // lanes
    ext, mid = rows + 4, rows + 2
    me = place_ref[0]
    for k in range(count):
        unit = jnp.bitwise_xor(k, me)
        canvas, a, b = unit // 4, (unit // 2) % 2, unit % 2

        @pl.loop(0, rows // 2 + 2)
        def _(i):
            start = (canvas * ext + 2 * i + a) * per_row + b * group
            grads[pl.ds(start, group)] = fold(blocks[k][pl.ds(pl.multiple_of(i * half, half), half), :].astype(F32))

    half_ref[...] = jnp.zeros_like(half_ref)
    for c in range(canvases):
        down_mask, up_mask = edge_masks(flag_ref, c, half, lanes)
        for row, flag in ((1, 1), (mid, 2)):

            @pl.when(flag_ref[c, flag] == 0)
            def _():
                grads[pl.ds((c * ext + row) * per_row, per_row)] = jnp.zeros((per_row, 8, width), F32)

        @pl.loop(0, mid)
        def _(r):
            normed, _ = normalise(inputs_ref[rows_at(c * ext + r + 1, grid), :].astype(F32))
            first = (normed * (1.0 + mods_ref[c, 1]) + mods_ref[c, 0]).astype(BF16).astype(F32)
            keep = jnp.where(r == 0, flag_ref[c, 1], jnp.where(r == mid - 1, flag_ref[c, 2], 1.0))
            base = (c * mid + r) * per_row
            cells[pl.ds(base, per_row)] = fold(first * keep)
            fill_sides(cells, side, down_mask, up_mask, base, chunks, lanes)
            fill_sides(grads, grads_side, down_mask, up_mask, (c * ext + r + 1) * per_row, chunks, lanes)

        @pl.loop(0, chunks)
        def _(k):
            cols = pl.ds(pl.multiple_of(k * lanes, lanes), lanes)
            taps = [spread_tap(kernel_ref, 8 - t, cols, lanes) for t in range(9)]

            def row_step(r, sums):
                load_grads = lambda down: load_row(grads, grads_side, (c * ext + r + 1 + down) * per_row, group, cols)
                back_even, back_odd = conv_row(load_grads, taps)
                here = (c * rows + r) * per_row
                back[pl.ds(here, group), :, cols] = back_even
                back[pl.ds(here + group, group), :, cols] = back_odd
                mine = (c * ext + r + 2) * per_row
                g_even = grads[pl.ds(mine, group), :, cols]
                g_odd = grads[pl.ds(mine + group, group), :, cols]
                new = []
                for down in range(3):
                    even, odd, odd_down, even_up = load_row(cells, side, (c * mid + r + down) * per_row, group, cols)
                    for for_even, for_odd in ((odd_down, even), (even, odd), (odd, even_up)):
                        new.append(jnp.sum(for_even * g_even + for_odd * g_odd, axis=0))
                new.append(jnp.sum(g_even + g_odd, axis=0))
                return tuple(s + v for s, v in zip(sums, new))

            sums = lax.fori_loop(0, rows, row_step, (jnp.zeros((8, lanes), F32),) * 10)
            for t in range(10):
                total = jnp.sum(sums[t], axis=0, keepdims=True)
                if c == 0:
                    sums_ref[pl.ds(t, 1), cols] = total
                else:
                    sums_ref[pl.ds(t, 1), cols] += total

        @pl.loop(0, rows)
        def _(r):
            normed, rate = normalise(inputs_ref[rows_at(c * ext + r + 2, grid), :].astype(F32))
            grad = back[pl.ds((c * rows + r) * per_row, per_row)].reshape(grid, width)
            half_ref[c, 0] += half_sums(grad)
            half_ref[c, 1] += half_sums(grad * normed)
            spots = rows_at(c * rows + r, grid)
            total = grad_hidden_ref[spots, :] + normalise_back(grad * (1.0 + mods_ref[c, 1]), normed, rate)
            result[spots, :] = total.astype(BF16)

    sorted_rows(result, out_ref, canvases * rows, grid, True)


def finish(flags, place, blocks, inputs, grad_hidden, kernel, mods, canvases, rows, half):
    own, width = grad_hidden.shape
    grid = 2 * half
    sizes = [canvases * n * grid // 8 for n in (rows + 2, rows + 4, rows)]
    return whole_call(
        functools.partial(finish_body, canvases, rows, half, len(blocks)),
        (flags, place, *blocks, inputs, grad_hidden, kernel, mods),
        (
            jax.ShapeDtypeStruct((own, width), BF16),
            jax.ShapeDtypeStruct((canvases, 2, 2, 8, width), F32),
            jax.ShapeDtypeStruct((16, width), F32),
        ),
        [pltpu.VMEM((sizes[0], 8, width), F32)] * 2
        + [pltpu.VMEM((sizes[1], 8, width), F32)] * 2
        + [pltpu.VMEM((sizes[2], 8, width), F32), pltpu.VMEM((own, width), BF16)],
        "finish",
        60 * own * width,
        scalars=2,
    )


def trade(blocks):
    size = lax.axis_size("fsdp")
    parts = [blocks[k] for k in range(size)]
    moved = {}
    for k in list(range(size - 1, 0, -1)):
        moved[k] = lax.ppermute(parts[k], "fsdp", [(i, i ^ k) for i in range(size)])
    return [parts[0]] + [moved[k] for k in range(1, size)]


def attention_grads_body(mixed_ref, part_ref, attended_ref, grad_ref, out_ref, left):
    step = pl.program_id(0)
    split = pl.num_programs(0) * 3 // 4

    @pl.when(step == 0)
    def _():
        left[...] = mixed_ref[...].T

    @pl.when(step == split)
    def _():
        left[...] = attended_ref[...].T

    @pl.when(step < split)
    def _():
        out_ref[...] = matmul(left[...], part_ref[0]).astype(BF16)

    @pl.when(step >= split)
    def _():
        out_ref[...] = matmul(left[...], grad_ref[...]).astype(BF16)


def attention_grads(mixed, parts, attended, grad_branch):
    tokens, width = mixed.shape
    tile = 256
    per = width // tile
    whole = pl.BlockSpec((tokens, width), lambda i: (0, 0), pipeline_mode=pl.Buffered(1))
    return pl.pallas_call(
        attention_grads_body,
        grid=(4 * per,),
        in_specs=[
            whole,
            pl.BlockSpec((1, tokens, tile), lambda i: (jnp.minimum(i // per, 2), 0, i % per)),
            whole,
            pl.BlockSpec((tokens, tile), lambda i: (0, jnp.maximum(i - 3 * per, 0))),
        ],
        out_specs=pl.BlockSpec((width, tile), lambda i: (0, i)),
        out_shape=jax.ShapeDtypeStruct((width, 4 * width), BF16),
        scratch_shapes=[pltpu.VMEM((width, tokens), BF16)],
        compiler_params=pltpu.CompilerParams(vmem_limit_bytes=32 << 20, dimension_semantics=("arbitrary",)),
        cost_estimate=pl.CostEstimate(flops=8 * tokens * width * width, bytes_accessed=14 << 20, transcendentals=0),
        name="attention_grads",
    )(mixed, parts, attended, grad_branch)


def per_device(
    tokens,
    cotangent,
    size_tags,
    step_ids,
    ada_weight,
    ada_bias,
    attn_kernel,
    attn_shift,
    qkv_weight,
    qv_bias,
    out_weight,
    out_bias,
    up_weight,
    up_bias,
    ffn_kernel,
    ffn_shift,
    down_weight,
    down_bias,
):
    canvases, rows, grid, width = tokens.shape[1:]
    half = grid // 2
    n_dp, n_fsdp = lax.axis_size("dp"), lax.axis_size("fsdp")
    count = n_dp * n_fsdp
    assert canvases * 4 == n_fsdp and rows * n_fsdp == grid
    fsdp_index = lax.axis_index("fsdp")
    every_bit = bits_of("fsdp") + bits_of("dp")
    hidden_units = up_weight.shape[1]
    shard = width // count
    ff_shard = hidden_units // count

    first_pair = lax.all_gather(
        jnp.concatenate([qkv_weight, out_weight], axis=1), EVERY, axis=0, tiled=True
    )
    out_full = first_pair[:, 3 * width :]
    up_rows = up_weight.reshape(shard, ff_shard * count // width, width).transpose(1, 0, 2)
    up_rows = up_rows.reshape(ff_shard, width)
    second_pair = lax.all_gather(
        jnp.concatenate([up_rows, down_weight], axis=0)[None], EVERY, axis=0, tiled=True
    )
    parts = [
        ada_bias,
        attn_kernel,
        attn_shift,
        qv_bias,
        out_bias,
        up_bias,
        ffn_kernel,
        ffn_shift,
        down_bias,
        size_tags,
        step_ids,
    ]
    packed = gather_small(
        jnp.concatenate([part.astype(F32).reshape(-1) for part in parts]), every_bit
    )
    pieces = []
    start = 0
    for part in parts:
        size = math.prod(part.shape)
        pieces.append(packed[:, start : start + size])
        start += size
    whole = [
        piece.reshape((count,) + part.shape).swapaxes(0, 1).reshape(part.shape[0], -1)
        if part.ndim == 2
        else piece.reshape(-1)
        for piece, part in zip(pieces[:9], parts[:9])
    ]
    (
        ada_bias_full,
        attn_kernel_full,
        attn_shift_full,
        qv_bias_full,
        out_bias_full,
        up_bias_full,
        ffn_kernel_full,
        ffn_shift_full,
        down_bias_full,
    ) = whole
    tags = pieces[9].reshape(n_dp, n_fsdp, canvases)[:, 0].reshape(n_dp * canvases)
    steps = pieces[10].reshape(n_dp, n_fsdp, canvases, 4)[:, 0].reshape(n_dp * canvases, 4)

    chosen = jnp.where(tags[:, None] == 1, steps[:, :1], steps).reshape(-1)
    device = lax.axis_index("dp") * n_fsdp + fsdp_index
    feature = device * shard + jnp.arange(shard)
    half_width = width // 2
    frequency = jnp.exp(
        -math.log(10000.0) * (feature % half_width).astype(F32) / half_width
    )
    angles = chosen[:, None] * frequency
    embedded = jnp.where(feature < half_width, jnp.cos(angles), jnp.sin(angles))
    embedded = jax.nn.silu(embedded).astype(BF16)
    modulation = matmul(embedded, ada_weight)
    for axis, bit in bits_of("fsdp"):
        keep, give = halves(modulation, my_bit(axis, bit), 1)
        modulation = keep + swap(give, axis, bit)
    for axis, bit in bits_of("dp")[::-1]:
        keep, give = halves(modulation, my_bit(axis, bit), 0)
        modulation = keep + swap(give, axis, bit)
    for axis, bit in bits_of("fsdp")[::-1]:
        modulation = by_bit(
            modulation, swap(modulation, axis, bit), my_bit(axis, bit), 1, jnp.concatenate
        )
    modulation = (modulation + ada_bias_full).reshape(canvases, 4, 6 * width)
    first_row = fsdp_index * rows
    row_half = (first_row >= half).astype(jnp.int32)
    local_mod = lax.dynamic_slice_in_dim(modulation, 2 * row_half, 2, axis=1)
    mods = local_mod.reshape(canvases, 2, 6, width).swapaxes(1, 2)
    mods = jnp.repeat(mods[:, :, None], 2, axis=2)
    mods = jnp.repeat(mods, half // 2, axis=3).reshape(canvases, 6, grid, width)

    big_item = size_tags[0] == 1
    big = big_item.astype(F32)
    edge = jnp.concatenate(
        [tokens[0][:, -2:], cotangent[0][:, -1:]], axis=1
    ), jnp.concatenate([tokens[0][:, :2], cotangent[0][:, :1]], axis=1)
    ends = n_fsdp - 1
    above = lax.ppermute(edge[0], "fsdp", [(i, i + 1) for i in range(ends)])
    below = lax.ppermute(edge[1], "fsdp", [(i + 1, i) for i in range(ends)])
    inputs = jnp.concatenate([above[:, :2], tokens[0], below[:, :2]], axis=1).reshape(-1, width)
    grad_out = jnp.concatenate([above[:, 2:], cotangent[0], below[:, 2:]], axis=1).reshape(-1, width)
    crosses_top = jnp.logical_and(first_row == half, jnp.logical_not(big_item))
    crosses_end = jnp.logical_and(first_row + rows == half, jnp.logical_not(big_item))
    top_ok = jnp.where(jnp.logical_or(fsdp_index == 0, crosses_top), 0.0, 1.0)
    end_ok = jnp.where(jnp.logical_or(fsdp_index == n_fsdp - 1, crosses_end), 0.0, 1.0)

    flags = jnp.stack([big, top_ok, end_ok], axis=1)

    unit_canvas, row_parity, col_parity = fsdp_index // 4, (fsdp_index // 2) % 2, fsdp_index % 2
    unit_big = jnp.take(big_item, unit_canvas)
    owners = jnp.arange(n_fsdp)
    middle_split = jnp.logical_not(unit_big)
    top_edge = jnp.logical_or(owners == 0, jnp.logical_and(owners == n_fsdp // 2, middle_split))
    end_edge = jnp.logical_or(
        owners == n_fsdp - 1, jnp.logical_and(owners == n_fsdp // 2 - 1, middle_split)
    )
    place = jnp.concatenate([jnp.stack([fsdp_index, row_parity]), top_edge, end_edge]).astype(jnp.int32)
    spots = jnp.arange(half)
    right_side = (spots >= half // 2).astype(jnp.int32)
    block_side = (jnp.bitwise_xor(owners, fsdp_index) >= n_fsdp // 2).astype(jnp.int32)
    quad = jnp.broadcast_to(
        (2 * block_side[:, None, None] + right_side), (n_fsdp, rows // 2, half)
    ).reshape(-1)
    lane = jnp.arange(128)[None]
    hot = quad[:, None] == lane
    query_item = hot.astype(BF16)
    open_keys = jnp.logical_or(unit_big, jnp.logical_or(hot, lane >= 4))
    key_item = jnp.where(open_keys, 0.0, -1e30).astype(BF16)

    attn_taps = jnp.pad(attn_kernel_full, ((0, 7), (0, 0)))
    inputs, grad_out, blocks = prepare(flags, place, inputs, grad_out, attn_taps, canvases, rows, half)
    blocks = trade(blocks)
    unit_mod = jnp.take(modulation, unit_canvas, axis=0).reshape(2, 2, 6, width)
    unit_mod = jnp.repeat(unit_mod, half // 2, axis=1)
    unit_shift, unit_scale = unit_mod[:, :, 0], 1.0 + unit_mod[:, :, 1]
    tap_grid = attn_kernel_full.reshape(3, 3, width)
    lost_row = jnp.take(tap_grid, 2 * row_parity, axis=0)
    at_side = jnp.where(
        col_parity == 0,
        jnp.logical_or(spots == 0, jnp.logical_and(spots == half // 2, middle_split)),
        jnp.logical_or(spots == half - 1, jnp.logical_and(spots == half // 2 - 1, middle_split)),
    )

    def taps_left(grid_part):
        lost = jnp.take(grid_part, 2 * col_parity, axis=1).sum(axis=0)
        return grid_part.sum(axis=(0, 1)) - jnp.where(at_side[:, None], lost, 0.0)

    full_taps = taps_left(tap_grid)
    edge_taps = full_taps - taps_left(lost_row[None])
    taps_here = jnp.stack([full_taps, edge_taps])
    unit_add = unit_shift[None] * taps_here[:, None] + attn_shift_full
    bias_row = jnp.concatenate([qv_bias_full[0], jnp.zeros((width,), F32), qv_bias_full[1]])
    mixed_unit, projected = project(
        place, blocks, unit_scale, unit_add.reshape(4, half, width), first_pair, bias_row[None], half
    )
    attended_unit, lse = attend_forward(place, projected, query_item, key_item, n_fsdp, half)
    second, hidden, branch_one, attended = middle(
        flags, place, trade(attended_unit), inputs, out_full, out_bias_full[None], mods, canvases, rows, half
    )

    gate_two = mods[:, 5][:, None]
    grad_two = (gate_two * grad_out.reshape(canvases, rows + 2, grid, width).astype(F32)).astype(BF16)
    branch_two, grad_second, ff_grads, ff_sums = feed_forward(
        flags,
        second,
        grad_two.reshape(-1, width),
        second_pair,
        up_bias_full,
        ffn_kernel_full,
        ffn_shift_full,
        canvases,
        rows,
        half,
    )
    grad_ffn_kernel, grad_ffn_shift, grad_up_bias = ff_sums[:9], ff_sums[9], ff_sums[10]
    ff_grads = lax.psum_scatter(ff_grads, EVERY, scatter_dimension=0, tiled=True)[0]
    grad_up = ff_grads[:ff_shard].reshape(ff_shard // shard, shard, width)
    grad_up = grad_up.transpose(1, 0, 2).reshape(shard, hidden_units).astype(F32)
    grad_down = ff_grads[ff_shard:].astype(F32)

    result, grad_hidden, grad_branch, blocks, late_sums, bias_sums = turn(
        place,
        branch_two,
        grad_second,
        hidden,
        branch_one,
        grad_out,
        out_full,
        down_bias_full[None],
        mods,
        canvases,
        rows,
        half,
    )
    bias_sums = jnp.sum(bias_sums, axis=1)
    grad_out_bias, grad_down_bias = bias_sums[0], bias_sums[1]
    grad_parts, part_sums = attend_backward(
        projected, query_item, key_item, trade(blocks), attended_unit, lse, half
    )
    part_sums = jnp.sum(part_sums, axis=1)
    grad_qv_bias = jnp.stack([part_sums[0], part_sums[2]])
    blocks = trade(project_back(place, grad_parts, first_pair, n_fsdp, half))
    attn_grads = attention_grads(mixed_unit, grad_parts, attended, grad_branch)
    attn_grads = lax.psum_scatter(attn_grads, EVERY, scatter_dimension=0, tiled=True)
    grad_qkv = attn_grads[:, : 3 * width].astype(F32)
    grad_out_weight = attn_grads[:, 3 * width :].astype(F32)
    grad_inputs, early_sums, tap_sums = finish(
        flags, place, blocks, inputs, grad_hidden, attn_taps, mods, canvases, rows, half
    )
    grad_attn_kernel, grad_attn_shift = tap_sums[:9], tap_sums[9]
    result = result.reshape(tokens.shape)
    grad_tokens = grad_inputs.reshape(tokens.shape)

    early_sums = jnp.sum(early_sums, axis=3)
    late_sums = jnp.sum(late_sums, axis=3)
    local_grad = jnp.concatenate(
        [early_sums[:, 0], early_sums[:, 1], late_sums[:, 0], late_sums[:, 1], late_sums[:, 2], late_sums[:, 3]],
        axis=-1,
    )
    fsdp_bits = bits_of("fsdp")
    for axis, bit in fsdp_bits[:-1]:
        local_grad = local_grad + swap(local_grad, axis, bit)
    mod_grads = gather_small(local_grad, fsdp_bits[-1:] + bits_of("dp"))
    mod_grads = mod_grads.reshape(n_dp, 2, canvases, 2, 6 * width).transpose(0, 2, 1, 3, 4)
    mod_grads = mod_grads.reshape(n_dp * canvases * 4, 6 * width)
    grad_ada = jnp.dot(embedded.astype(F32).T, mod_grads, precision=lax.Precision.HIGHEST)
    bias_size = ada_bias.shape[0]
    grad_ada_bias = lax.dynamic_slice_in_dim(
        jnp.sum(mod_grads, axis=0), device * bias_size, bias_size
    )

    smalls = [
        grad_attn_kernel,
        grad_attn_shift,
        grad_qv_bias,
        grad_out_bias,
        grad_up_bias,
        grad_ffn_kernel,
        grad_ffn_shift,
        grad_down_bias,
    ]
    blocks = []
    for small in smalls:
        if small.ndim == 1:
            blocks.append(small.reshape(count, -1))
        else:
            lead = small.shape[0]
            blocks.append(small.reshape(lead, count, -1).swapaxes(0, 1).reshape(count, -1))
    summed = scatter_small(jnp.concatenate(blocks, axis=1), every_bit)[0]
    small_grads = []
    start = 0
    for small in smalls:
        size = math.prod(small.shape) // count
        piece = summed[start : start + size]
        small_grads.append(piece if small.ndim == 1 else piece.reshape(small.shape[0], -1))
        start += size
    (
        grad_attn_kernel,
        grad_attn_shift,
        grad_qv_bias,
        grad_out_bias,
        grad_up_bias,
        grad_ffn_kernel,
        grad_ffn_shift,
        grad_down_bias,
    ) = small_grads
    return (
        result,
        grad_tokens,
        grad_ada,
        grad_ada_bias,
        grad_attn_kernel,
        grad_attn_shift,
        grad_qkv,
        grad_qv_bias,
        grad_out_weight,
        grad_out_bias,
        grad_up,
        grad_up_bias,
        grad_ffn_kernel,
        grad_ffn_shift,
        grad_down,
        grad_down_bias,
    )


def solution(mesh):
    cells = P("dp", None, "fsdp", None, None)
    by_row = P(EVERY, None)
    by_col = P(None, EVERY)
    flat = P(EVERY)
    weights = (by_row, flat, by_col, flat, by_row, by_col, by_row, flat, by_row, flat, by_col, flat, by_row, flat)
    return jax.shard_map(
        per_device,
        mesh=mesh,
        in_specs=(cells, cells, P("dp", None), P("dp", None, None)) + weights,
        out_specs=(cells, cells) + weights,
        check_vma=False,
    )
```
